256 devices in a mesh: ka: 32 (over z, y_lo, core), ga: 8 (over x, y_hi).
Axes of the slice: x: 4, y: 4 (y_hi: 2, y_lo: 2; y = y_hi * 2 + y_lo), z: 8, core: 2. Of those that a mesh axis runs over, the one named last changes fastest.
Arguments:
- offsets: int32 [2], replicated, may hold values from 0 to 31
- q_slots: int32 [32], replicated, may hold values from 0 to 31, each once
- forms: bfloat16 [1024, 128, 512], P('ka', None, 'ga'), may hold values from -0.25 to 0.25
- vectors: bfloat16 [1024, 32, 128], P('ka'), may hold values from -6 to 6
- energies: float32 [1024, 128], P('ka'), may hold values from 0.5 to 2
- screened: bfloat16 [32, 512, 32, 512], P('ka', 'ga'), may hold values from -0.046875 to 0.046875
- umklapp: int32 [32, 32, 512], P('ka'), may hold values from 0 to 511, as said below
Outputs:
- applied: float32 [1024, 32, 128], P('ka')
The draws below stay inside these ranges and needn't reach their ends.
Inputs may be any that keep to these rules, and one draw needn't show every extreme that they name: Each row umklapp[qx, s, :] holds every value of 0 to 511 once. `q_slots`: each slot's value appears once.
All inputs are finite; a program needn't handle non-finite values.
Results may differ from the reference program's by a relative error of at most 0.0025.
Values may be sent and summed in bfloat16 or wider, within the bound.
A program may use at most 128 MiB of HBM per device.

```python
import jax
import jax.numpy as jnp
from jax import lax

NG = 512
NKY = 32
NB = 32
STEPS = 2
NKX = 32
NK = 1024
NT = 128


def draw_umklapp(key, part):
    splits = jax.random.split(jax.random.fold_in(key, 17), NKX * NKY)

    def one_order(single):
        return jax.random.permutation(single, NG)
    orders = jax.vmap(one_order)(splits)
    return orders.reshape(NKX, NKY, NG).astype(jnp.int32)


def level_of(own_key, dims, cuts, low, high):
    def one(axis_at, blocks):
        heights = jax.random.uniform(jax.random.fold_in(jax.random.fold_in(own_key, 6), axis_at), (blocks,), jnp.float32, low / len(cuts), high / len(cuts))
        return jnp.repeat(jnp.exp(heights), dims[axis_at] // blocks).reshape((-1,) + (1,) * (len(dims) - axis_at - 1))

    loudness = one(*cuts[0])
    for cut in cuts[1:]:
        loudness = loudness * one(*cut)
    return loudness


def noise(rng, dims, spread, most, cuts=(), kind=jnp.bfloat16):
    array = spread * jax.random.normal(rng, dims, jnp.float32)
    if cuts:
        array = array * level_of(rng, dims, cuts, -0.22, 0.18)
    return jnp.clip(array, -most, most).astype(kind)


def setup_inputs(seed: int = 0) -> dict:
    arg_keys = jax.random.split(jax.random.key(seed), 8)
    return {
        "offsets": jax.random.randint(arg_keys[0], (STEPS,), 0, NKX).astype(jnp.int32),
        "q_slots": jax.random.permutation(arg_keys[1], NKY).astype(jnp.int32),
        "forms": noise(arg_keys[2], (NK, NT, NG), NG ** -0.5, 0.25, ((0, 32), (2, 8))),
        "vectors": noise(arg_keys[3], (NK, NB, NT), 1.0, 6.0, ((0, 32),)),
        "energies": jnp.clip(0.5 + 1.5 * jax.random.uniform(arg_keys[4], (NK, NT), jnp.float32) ** level_of(arg_keys[4], (NK, NT), ((0, 32),), -0.2, 0.2), 0.5, 2.0),
        "screened": noise(arg_keys[5], (NKX, NG, NKY, NG), (NKY * NG) ** -0.5, 0.046875, ((0, 32), (1, 8))),
        "umklapp": draw_umklapp(jax.random.fold_in(arg_keys[7], 71), 0),
    }


def reference(offsets, q_slots, forms, vectors, energies, screened, umklapp):
    forms_wide = forms.astype(jnp.float32)
    vectors_wide = vectors.astype(jnp.float32)
    projected = jnp.einsum("kbt,ktg->kbg", vectors_wide, forms_wide).astype(jnp.bfloat16)
    projected_wide = lax.optimization_barrier(projected).astype(jnp.float32)
    blocks = projected_wide.reshape(NKX, NKY, NB, NG)
    forms_rows = forms_wide.reshape(NKX, NKY, NT, NG)
    positions = jnp.arange(NKY, dtype=jnp.int32)
    slot_index = (positions[None, :] - q_slots[:, None]) % NKY
    slot_rows = jnp.arange(NKY, dtype=jnp.int32)[:, None]
    accumulated = jnp.zeros((NKX, NKY, NB, NT), jnp.float32)
    for step in range(STEPS):
        offset = offsets[step]
        moved = jnp.roll(blocks, offset, axis=0)
        screen_slab = lax.dynamic_index_in_dim(screened, offset, 0, keepdims=False).astype(jnp.float32)
        shift_table = lax.dynamic_index_in_dim(umklapp, offset, 0, keepdims=False)
        permuted = jnp.zeros_like(screen_slab).at[:, slot_rows, shift_table].set(screen_slab)
        matrix = permuted.reshape(NG * NKY, NG)

        def one_row(pair):
            moved_row, forms_row = pair
            products = jnp.dot(matrix, moved_row.reshape(NKY * NB, NG).T, preferred_element_type=jnp.float32)
            products = products.reshape(NG, NKY, NKY, NB)
            picked = jnp.take_along_axis(products, slot_index[None, :, :, None], axis=2)
            kernel_part = jnp.sum(picked, axis=1).astype(jnp.bfloat16)
            kernel_wide = lax.optimization_barrier(kernel_part).astype(jnp.float32)
            return jnp.einsum("gkb,ktg->kbt", kernel_wide, forms_row)

        accumulated = accumulated + lax.map(one_row, (moved, forms_rows))
    action = accumulated.reshape(NK, NB, NT)
    return energies[:, None, :] * vectors_wide - action
```

```python
import jax
import jax.numpy as jnp
from jax import lax
from jax.sharding import PartitionSpec as P


def from_behind(value, axis, by):
    count = lax.axis_size(axis)
    return lax.ppermute(value, axis, [(i, (i + by) % count) for i in range(count)])


def swap(value, axis, bit):
    count = lax.axis_size(axis)
    return lax.ppermute(value, axis, [(i, i ^ bit) for i in range(count)])


def pick_half(tree, axis_at, which):
    return jax.tree.map(lambda a: lax.dynamic_slice_in_dim(a, which, 1, axis=axis_at), tree)


def scatter_from_roots(own, roots, axis, order):
    nbits = len(order)
    me = lax.axis_index(axis)
    full = (1 << nbits) - 1
    held = [own] * len(roots)
    shared = True
    done_mask = 0
    for bit in order:
        axis_at = nbits - 1 - bit
        mine = (me >> bit) & 1
        if shared:
            sends = pick_half(own, axis_at, 1 - mine)
            got = swap(sends, axis, 1 << bit)
            got = [got] * len(roots)
        else:
            sends = [pick_half(h, axis_at, 1 - mine) for h in held]
            got = swap(sends, axis, 1 << bit)
        new_held = []
        for r, root in enumerate(roots):
            holder = ((me ^ root) & (full & ~done_mask)) == 0
            keep = pick_half(held[r], axis_at, mine)
            new_held.append(
                jax.tree.map(lambda k, g: jnp.where(holder, k, g), keep, got[r])
            )
        held = new_held
        shared = False
        done_mask |= 1 << bit
    return held


def gather_all(pieces, axis, order):
    nbits = len(order)
    me = lax.axis_index(axis)
    held = pieces
    for bit in order:
        axis_at = nbits - 1 - bit
        mine = (me >> bit) & 1
        got = swap(held, axis, 1 << bit)

        def join(h, g):
            low = jnp.where(mine == 0, h, g)
            high = jnp.where(mine == 0, g, h)
            return jnp.concatenate([low, high], axis=axis_at)

        held = jax.tree.map(join, held, got)
    return held


def sum_all(value, axis, order):
    nbits = len(order)
    me = lax.axis_index(axis)
    held = value
    for bit in order:
        axis_at = nbits - 1 - bit
        mine = (me >> bit) & 1
        sends = lax.dynamic_slice_in_dim(held, 1 - mine, 1, axis=axis_at)
        keep = lax.dynamic_slice_in_dim(held, mine, 1, axis=axis_at)
        held = keep + swap(sends, axis, 1 << bit)
    return gather_all(held, axis, order[::-1])


def body(offsets, q_slots, forms, vectors, energies, screened, umklapp):
    kpoint_count = vectors.shape[0]
    vector_count = vectors.shape[1]
    pair_count = vectors.shape[2]
    local_waves = forms.shape[2]
    slot_count = screened.shape[2]
    plane_waves = screened.shape[3]
    step_count = offsets.shape[0]
    ka_size = lax.axis_size("ka")
    ga_size = lax.axis_size("ga")
    ka_bits = ka_size.bit_length() - 1
    ga_bits = ga_size.bit_length() - 1
    me_ka = lax.axis_index("ka")

    projected = lax.dot_general(
        vectors, forms, (((2,), (1,)), ((0,), (0,))), preferred_element_type=jnp.float32
    ).astype(jnp.bfloat16)

    per_piece = slot_count // ka_size
    slab = jnp.transpose(screened[0], (1, 0, 2))
    slab = slab.reshape((2,) * ka_bits + (per_piece, local_waves, plane_waves))
    table = umklapp[0].reshape((2,) * ka_bits + (per_piece, plane_waves))
    roots = [offsets[i] for i in range(step_count)]
    pieces = scatter_from_roots((slab, table), roots, "ka", list(range(ka_bits)))
    waves = jnp.arange(plane_waves, dtype=jnp.int32)
    permuted_pieces = []
    for piece, rows in pieces:
        piece = piece.reshape(per_piece, local_waves, plane_waves)
        rows = rows.reshape(per_piece, plane_waves)
        onehot = (rows[:, :, None] == waves[None, None, :]).astype(jnp.bfloat16)
        moved_cols = lax.dot_general(
            piece, onehot, (((2,), (1,)), ((0,), (0,))), preferred_element_type=jnp.float32
        ).astype(jnp.bfloat16)
        permuted_pieces.append(
            moved_cols.reshape((1,) * ka_bits + (per_piece, local_waves, plane_waves))
        )
    gathered = gather_all(permuted_pieces, "ka", list(range(ka_bits))[::-1])

    moving = [projected] * step_count
    for level in range(ka_bits):
        hopped = from_behind(jnp.stack(moving), "ka", 1 << level)
        moving = [
            jnp.where(roots[i] >> level & 1 == 1, hopped[i], moving[i])
            for i in range(step_count)
        ]
    moving_all = lax.all_gather(jnp.stack(moving), "ga", axis=3, tiled=True)

    positions = jnp.arange(kpoint_count, dtype=jnp.int32)
    slot_index = (positions[None, :] - q_slots[:, None]) % kpoint_count
    parts = []
    for step in range(step_count):
        permuted = gathered[step].reshape(slot_count, local_waves, plane_waves)
        products = lax.dot_general(
            permuted,
            moving_all[step],
            (((2,), (2,)), ((), ())),
            preferred_element_type=jnp.float32,
        )
        picked = jnp.take_along_axis(products, slot_index[:, None, :, None], axis=2)
        parts.append(jnp.sum(picked, axis=0).astype(jnp.bfloat16))
    kernel_cat = jnp.concatenate(parts, axis=2)
    action = lax.dot_general(
        kernel_cat, forms, (((0,), (2,)), ((1,), (0,))), preferred_element_type=jnp.float32
    )
    action = action.reshape(kpoint_count, step_count, vector_count, pair_count).sum(axis=1)
    ga_order = [1, 0, 2][:ga_bits] if ga_bits == 3 else list(range(ga_bits))
    action = action.reshape((2,) * ga_bits + (kpoint_count // ga_size, vector_count, pair_count))
    action = sum_all(action, "ga", ga_order).reshape(kpoint_count, vector_count, pair_count)
    return energies[:, None, :] * vectors.astype(jnp.float32) - action


def solution(mesh):
    return jax.shard_map(
        body,
        mesh=mesh,
        in_specs=(
            P(),
            P(),
            P("ka", None, "ga"),
            P("ka", None, None),
            P("ka", None),
            P("ka", "ga", None, None),
            P("ka", None, None),
        ),
        out_specs=P("ka", None, None),
        check_vma=False,
    )
```

```python
import functools

import jax
import jax.numpy as jnp
from jax import lax
from jax.experimental import pallas as pl
from jax.experimental.pallas import tpu as pltpu
from jax.sharding import PartitionSpec as P


def from_behind(value, axis, by):
    count = lax.axis_size(axis)
    return lax.ppermute(value, axis, [(i, (i + by) % count) for i in range(count)])


def swap(value, axis, bit):
    count = lax.axis_size(axis)
    return lax.ppermute(value, axis, [(i, i ^ bit) for i in range(count)])


def pick_half(tree, axis_at, which):
    return jax.tree.map(lambda a: lax.dynamic_slice_in_dim(a, which, 1, axis=axis_at), tree)


def scatter_from_roots(own, roots, axis, order):
    nbits = len(order)
    me = lax.axis_index(axis)
    full = (1 << nbits) - 1
    held = [own] * len(roots)
    shared = True
    done_mask = 0
    for bit in order:
        axis_at = nbits - 1 - bit
        mine = (me >> bit) & 1
        if shared:
            sends = pick_half(own, axis_at, 1 - mine)
            got = swap(sends, axis, 1 << bit)
            got = [got] * len(roots)
        else:
            sends = [pick_half(h, axis_at, 1 - mine) for h in held]
            got = swap(sends, axis, 1 << bit)
        new_held = []
        for r, root in enumerate(roots):
            holder = ((me ^ root) & (full & ~done_mask)) == 0
            keep = pick_half(held[r], axis_at, mine)
            new_held.append(
                jax.tree.map(lambda k, g: jnp.where(holder, k, g), keep, got[r])
            )
        held = new_held
        shared = False
        done_mask |= 1 << bit
    return held


def gather_all(pieces, axis, order):
    nbits = len(order)
    me = lax.axis_index(axis)
    held = pieces
    for bit in order:
        axis_at = nbits - 1 - bit
        mine = (me >> bit) & 1
        got = swap(held, axis, 1 << bit)

        def join(h, g):
            low = jnp.where(mine == 0, h, g)
            high = jnp.where(mine == 0, g, h)
            return jnp.concatenate([low, high], axis=axis_at)

        held = jax.tree.map(join, held, got)
    return held


def sum_all(value, axis, order):
    nbits = len(order)
    me = lax.axis_index(axis)
    held = value
    for bit in order:
        axis_at = nbits - 1 - bit
        mine = (me >> bit) & 1
        sends = lax.dynamic_slice_in_dim(held, 1 - mine, 1, axis=axis_at)
        keep = lax.dynamic_slice_in_dim(held, mine, 1, axis=axis_at)
        held = keep + swap(sends, axis, 1 << bit)
    return gather_all(held, axis, order[::-1])


def contract_kernel(block, q_ref, perm_ref, mov_ref, out_ref, acc_ref):
    slots = perm_ref.shape[1]
    rows = out_ref.shape[1]
    count = rows // block
    acc_ref[...] = jnp.zeros_like(acc_ref)

    def one_slot(s, carry):
        start = pl.multiple_of((count - q_ref[s]) * block, block)
        rolled = mov_ref[0, pl.ds(start, rows), :]
        acc_ref[...] += lax.dot_general(
            rolled, perm_ref[0, s], (((1,), (1,)), ((), ())),
            preferred_element_type=jnp.float32,
        )
        return carry

    lax.fori_loop(0, slots, one_slot, 0)
    out_ref[0] = acc_ref[...].astype(out_ref.dtype)


def contract(q_slots, permuted, doubled, block):
    steps, slots, local, waves = permuted.shape
    rows = doubled.shape[1] // 2
    return pl.pallas_call(
        functools.partial(contract_kernel, block),
        out_shape=jax.ShapeDtypeStruct((steps, rows, local), jnp.bfloat16),
        grid_spec=pltpu.PrefetchScalarGridSpec(
            num_scalar_prefetch=1,
            grid=(steps,),
            in_specs=[
                pl.BlockSpec((1, slots, local, waves), lambda i, q: (i, 0, 0, 0)),
                pl.BlockSpec((1, 2 * rows, waves), lambda i, q: (i, 0, 0)),
            ],
            out_specs=pl.BlockSpec((1, rows, local), lambda i, q: (i, 0, 0)),
            scratch_shapes=[pltpu.VMEM((rows, local), jnp.float32)],
        ),
        cost_estimate=pl.CostEstimate(
            flops=2 * steps * slots * rows * local * waves,
            bytes_accessed=2 * steps * (slots * local * waves + 2 * rows * waves + rows * local),
            transcendentals=0,
        ),
    )(q_slots, permuted, doubled)


def body(offsets, q_slots, forms, vectors, energies, screened, umklapp):
    kpoint_count = vectors.shape[0]
    vector_count = vectors.shape[1]
    pair_count = vectors.shape[2]
    local_waves = forms.shape[2]
    slot_count = screened.shape[2]
    plane_waves = screened.shape[3]
    step_count = offsets.shape[0]
    ka_size = lax.axis_size("ka")
    ga_size = lax.axis_size("ga")
    ka_bits = ka_size.bit_length() - 1
    ga_bits = ga_size.bit_length() - 1
    me_ka = lax.axis_index("ka")

    projected = lax.dot_general(
        vectors, forms, (((2,), (1,)), ((0,), (0,))), preferred_element_type=jnp.float32
    ).astype(jnp.bfloat16)

    per_piece = slot_count // ka_size
    slab = jnp.transpose(screened[0], (1, 0, 2))
    slab = slab.reshape((2,) * ka_bits + (per_piece, local_waves, plane_waves))
    table = umklapp[0].reshape((2,) * ka_bits + (per_piece, plane_waves))
    roots = [offsets[i] for i in range(step_count)]
    pieces = scatter_from_roots((slab, table), roots, "ka", list(range(ka_bits)))
    waves = jnp.arange(plane_waves, dtype=jnp.int32)
    permuted_pieces = []
    for piece, rows in pieces:
        piece = piece.reshape(per_piece, local_waves, plane_waves)
        rows = rows.reshape(per_piece, plane_waves)
        onehot = (rows[:, :, None] == waves[None, None, :]).astype(jnp.bfloat16)
        moved_cols = lax.dot_general(
            piece, onehot, (((2,), (1,)), ((0,), (0,))), preferred_element_type=jnp.float32
        ).astype(jnp.bfloat16)
        permuted_pieces.append(
            moved_cols.reshape((1,) * ka_bits + (per_piece, local_waves, plane_waves))
        )
    gathered = gather_all(permuted_pieces, "ka", list(range(ka_bits))[::-1])

    moving = [projected] * step_count
    for level in range(ka_bits):
        hopped = from_behind(jnp.stack(moving), "ka", 1 << level)
        moving = [
            jnp.where(roots[i] >> level & 1 == 1, hopped[i], moving[i])
            for i in range(step_count)
        ]
    moving_all = lax.all_gather(jnp.stack(moving), "ga", axis=3, tiled=True)

    permuted_all = jnp.stack(
        [gathered[i].reshape(slot_count, local_waves, plane_waves) for i in range(step_count)]
    )
    moving_rows = moving_all.reshape(step_count, kpoint_count * vector_count, plane_waves)
    doubled = jnp.concatenate([moving_rows, moving_rows], axis=1)
    kernel_part = contract(q_slots, permuted_all, doubled, vector_count)
    kernel_part = kernel_part.reshape(step_count, kpoint_count, vector_count, local_waves)
    kernel_cat = jnp.concatenate([kernel_part[i] for i in range(step_count)], axis=1)
    action = lax.dot_general(
        kernel_cat, forms, (((2,), (2,)), ((0,), (0,))), preferred_element_type=jnp.float32
    )
    action = action.reshape(kpoint_count, step_count, vector_count, pair_count).sum(axis=1)
    ga_order = [1, 0, 2][:ga_bits] if ga_bits == 3 else list(range(ga_bits))
    action = action.reshape((2,) * ga_bits + (kpoint_count // ga_size, vector_count, pair_count))
    action = sum_all(action, "ga", ga_order).reshape(kpoint_count, vector_count, pair_count)
    return energies[:, None, :] * vectors.astype(jnp.float32) - action


def solution(mesh):
    return jax.shard_map(
        body,
        mesh=mesh,
        in_specs=(
            P(),
            P(),
            P("ka", None, "ga"),
            P("ka", None, None),
            P("ka", None),
            P("ka", "ga", None, None),
            P("ka", None, None),
        ),
        out_specs=P("ka", None, None),
        check_vma=False,
    )
```

```python
import functools

import jax
import jax.numpy as jnp
from jax import lax
from jax.experimental import pallas as pl
from jax.experimental.pallas import tpu as pltpu
from jax.sharding import PartitionSpec as P


def from_behind(value, axis, by):
    count = lax.axis_size(axis)
    return lax.ppermute(value, axis, [(i, (i + by) % count) for i in range(count)])


def swap(value, axis, bit):
    count = lax.axis_size(axis)
    return lax.ppermute(value, axis, [(i, i ^ bit) for i in range(count)])


def pick_half(tree, axis_at, which):
    return jax.tree.map(lambda a: lax.dynamic_slice_in_dim(a, which, 1, axis=axis_at), tree)


def scatter_from_roots(own, roots, axis, order):
    nbits = len(order)
    me = lax.axis_index(axis)
    full = (1 << nbits) - 1
    held = [own] * len(roots)
    shared = True
    done_mask = 0
    for bit in order:
        axis_at = nbits - 1 - bit
        mine = (me >> bit) & 1
        if shared:
            sends = pick_half(own, axis_at, 1 - mine)
            got = swap(sends, axis, 1 << bit)
            got = [got] * len(roots)
        else:
            sends = [pick_half(h, axis_at, 1 - mine) for h in held]
            stacked = jax.tree.map(lambda *xs: jnp.stack(xs), *sends)
            stacked = swap(stacked, axis, 1 << bit)
            got = [jax.tree.map(lambda x: x[r], stacked) for r in range(len(roots))]
        new_held = []
        for r, root in enumerate(roots):
            holder = ((me ^ root) & (full & ~done_mask)) == 0
            keep = pick_half(held[r], axis_at, mine)
            new_held.append(
                jax.tree.map(lambda k, g: jnp.where(holder, k, g), keep, got[r])
            )
        held = new_held
        shared = False
        done_mask |= 1 << bit
    return held


def gather_all(pieces, axis, order, lead=0):
    nbits = len(order)
    me = lax.axis_index(axis)
    held = pieces
    for bit in order:
        axis_at = lead + nbits - 1 - bit
        mine = (me >> bit) & 1
        got = swap(held, axis, 1 << bit)

        def join(h, g):
            low = jnp.where(mine == 0, h, g)
            high = jnp.where(mine == 0, g, h)
            return jnp.concatenate([low, high], axis=axis_at)

        held = jax.tree.map(join, held, got)
    return held


def sum_all(value, axis, order):
    nbits = len(order)
    me = lax.axis_index(axis)
    held = value
    for bit in order:
        axis_at = nbits - 1 - bit
        mine = (me >> bit) & 1
        sends = lax.dynamic_slice_in_dim(held, 1 - mine, 1, axis=axis_at)
        keep = lax.dynamic_slice_in_dim(held, mine, 1, axis=axis_at)
        held = keep + swap(sends, axis, 1 << bit)
    return gather_all(held, axis, order[::-1])


def contract_kernel(block, q_ref, perm_ref, mov_ref, out_ref, acc_ref):
    slots = perm_ref.shape[1]
    rows = out_ref.shape[1]
    acc_ref[...] = jnp.zeros_like(acc_ref)

    def one_slot(s, carry):
        start = pl.multiple_of(q_ref[s] * block, block)
        acc_ref[pl.ds(start, rows), :] += lax.dot_general(
            mov_ref[0], perm_ref[0, s], (((1,), (1,)), ((), ())),
            preferred_element_type=jnp.float32,
        )
        return carry

    lax.fori_loop(0, slots, one_slot, 0)
    out_ref[0] = (acc_ref[:rows, :] + acc_ref[rows:, :]).astype(out_ref.dtype)


def contract(q_slots, permuted, moving, block):
    steps, slots, local, waves = permuted.shape
    rows = moving.shape[1]
    return pl.pallas_call(
        functools.partial(contract_kernel, block),
        out_shape=jax.ShapeDtypeStruct((steps, rows, local), jnp.bfloat16),
        grid_spec=pltpu.PrefetchScalarGridSpec(
            num_scalar_prefetch=1,
            grid=(steps,),
            in_specs=[
                pl.BlockSpec((1, slots, local, waves), lambda i, q: (i, 0, 0, 0)),
                pl.BlockSpec((1, rows, waves), lambda i, q: (i, 0, 0)),
            ],
            out_specs=pl.BlockSpec((1, rows, local), lambda i, q: (i, 0, 0)),
            scratch_shapes=[pltpu.VMEM((2 * rows, local), jnp.float32)],
        ),
        cost_estimate=pl.CostEstimate(
            flops=2 * steps * slots * rows * local * waves,
            bytes_accessed=2 * steps * (slots * local * waves + rows * waves + rows * local),
            transcendentals=0,
        ),
    )(q_slots, permuted, moving)


def body(offsets, q_slots, forms, vectors, energies, screened, umklapp):
    kpoint_count = vectors.shape[0]
    vector_count = vectors.shape[1]
    pair_count = vectors.shape[2]
    local_waves = forms.shape[2]
    slot_count = screened.shape[2]
    plane_waves = screened.shape[3]
    step_count = offsets.shape[0]
    ka_size = lax.axis_size("ka")
    ga_size = lax.axis_size("ga")
    ka_bits = ka_size.bit_length() - 1
    ga_bits = ga_size.bit_length() - 1
    me_ka = lax.axis_index("ka")

    projected = lax.dot_general(
        vectors, forms, (((2,), (1,)), ((0,), (0,))), preferred_element_type=jnp.float32
    ).astype(jnp.bfloat16)

    per_piece = slot_count // ka_size
    slab = jnp.transpose(screened[0], (1, 0, 2))
    slab = slab.reshape((2,) * ka_bits + (per_piece, local_waves, plane_waves))
    table = umklapp[0].reshape((2,) * ka_bits + (per_piece, plane_waves))
    roots = [offsets[i] for i in range(step_count)]
    pieces = scatter_from_roots((slab, table), roots, "ka", list(range(ka_bits)))
    waves = jnp.arange(plane_waves, dtype=jnp.int32)
    permuted_pieces = []
    for piece, rows in pieces:
        piece = piece.reshape(per_piece, local_waves, plane_waves)
        rows = rows.reshape(per_piece, plane_waves)
        onehot = (rows[:, :, None] == waves[None, None, :]).astype(jnp.bfloat16)
        moved_cols = lax.dot_general(
            piece, onehot, (((2,), (1,)), ((0,), (0,))), preferred_element_type=jnp.float32
        ).astype(jnp.bfloat16)
        permuted_pieces.append(
            moved_cols.reshape((1,) * ka_bits + (per_piece, local_waves, plane_waves))
        )
    gathered = gather_all(jnp.stack(permuted_pieces), "ka", list(range(ka_bits))[::-1], lead=1)

    moving = [projected] * step_count
    for level in range(ka_bits):
        hopped = from_behind(jnp.stack(moving), "ka", 1 << level)
        moving = [
            jnp.where(roots[i] >> level & 1 == 1, hopped[i], moving[i])
            for i in range(step_count)
        ]
    moving_all = lax.all_gather(jnp.stack(moving), "ga", axis=3, tiled=True)

    permuted_all = gathered.reshape(step_count, slot_count, local_waves, plane_waves)
    moving_rows = moving_all.reshape(step_count, kpoint_count * vector_count, plane_waves)
    kernel_part = contract(q_slots, permuted_all, moving_rows, vector_count)
    kernel_part = kernel_part.reshape(step_count, kpoint_count, vector_count, local_waves)
    kernel_cat = jnp.concatenate([kernel_part[i] for i in range(step_count)], axis=1)
    action = lax.dot_general(
        kernel_cat, forms, (((2,), (2,)), ((0,), (0,))), preferred_element_type=jnp.float32
    )
    action = action.reshape(kpoint_count, step_count, vector_count, pair_count).sum(axis=1)
    ga_order = [1, 0, 2][:ga_bits] if ga_bits == 3 else list(range(ga_bits))
    action = action.reshape((2,) * ga_bits + (kpoint_count // ga_size, vector_count, pair_count))
    action = sum_all(action, "ga", ga_order).reshape(kpoint_count, vector_count, pair_count)
    return energies[:, None, :] * vectors.astype(jnp.float32) - action


def solution(mesh):
    return jax.shard_map(
        body,
        mesh=mesh,
        in_specs=(
            P(),
            P(),
            P("ka", None, "ga"),
            P("ka", None, None),
            P("ka", None),
            P("ka", "ga", None, None),
            P("ka", None, None),
        ),
        out_specs=P("ka", None, None),
        check_vma=False,
    )
```

```python
import functools

import jax
import jax.numpy as jnp
from jax import lax
from jax.experimental import pallas as pl
from jax.experimental.pallas import tpu as pltpu
from jax.sharding import PartitionSpec as P


def from_behind(value, axis, by):
    count = lax.axis_size(axis)
    return lax.ppermute(value, axis, [(i, (i + by) % count) for i in range(count)])


def swap(value, axis, bit):
    count = lax.axis_size(axis)
    return lax.ppermute(value, axis, [(i, i ^ bit) for i in range(count)])


def pick_half(tree, axis_at, which):
    return jax.tree.map(lambda a: lax.dynamic_slice_in_dim(a, which, 1, axis=axis_at), tree)


def scatter_from_roots(own, roots, axis, order):
    nbits = len(order)
    me = lax.axis_index(axis)
    full = (1 << nbits) - 1
    held = [own] * len(roots)
    shared = True
    done_mask = 0
    for bit in order:
        axis_at = nbits - 1 - bit
        mine = (me >> bit) & 1
        if shared:
            sends = pick_half(own, axis_at, 1 - mine)
            got = swap(sends, axis, 1 << bit)
            got = [got] * len(roots)
        else:
            sends = [pick_half(h, axis_at, 1 - mine) for h in held]
            stacked = jax.tree.map(lambda *xs: jnp.stack(xs), *sends)
            stacked = swap(stacked, axis, 1 << bit)
            got = [jax.tree.map(lambda x: x[r], stacked) for r in range(len(roots))]
        new_held = []
        for r, root in enumerate(roots):
            holder = ((me ^ root) & (full & ~done_mask)) == 0
            keep = pick_half(held[r], axis_at, mine)
            new_held.append(
                jax.tree.map(lambda k, g: jnp.where(holder, k, g), keep, got[r])
            )
        held = new_held
        shared = False
        done_mask |= 1 << bit
    return held


def gather_all(pieces, axis, order, lead=0):
    nbits = len(order)
    me = lax.axis_index(axis)
    held = pieces
    for bit in order:
        axis_at = lead + nbits - 1 - bit
        mine = (me >> bit) & 1
        got = swap(held, axis, 1 << bit)

        def join(h, g):
            low = jnp.where(mine == 0, h, g)
            high = jnp.where(mine == 0, g, h)
            return jnp.concatenate([low, high], axis=axis_at)

        held = jax.tree.map(join, held, got)
    return held


def sum_all(value, axis, order):
    nbits = len(order)
    me = lax.axis_index(axis)
    held = value
    for bit in order:
        axis_at = nbits - 1 - bit
        mine = (me >> bit) & 1
        sends = lax.dynamic_slice_in_dim(held, 1 - mine, 1, axis=axis_at)
        keep = lax.dynamic_slice_in_dim(held, mine, 1, axis=axis_at)
        held = keep + swap(sends, axis, 1 << bit)
    return gather_all(held, axis, order[::-1])


def contract_kernel(block, q_ref, perm_ref, mov_ref, out_ref):
    slots = perm_ref.shape[1]

    def one_slot(s, acc):
        product = jnp.dot(perm_ref[0, s], mov_ref[0], preferred_element_type=jnp.float32)
        return acc + pltpu.roll(product, q_ref[s] * block, 1)

    acc = lax.fori_loop(0, slots, one_slot, jnp.zeros(out_ref.shape[1:], jnp.float32))
    out_ref[0] = acc.astype(out_ref.dtype)


def contract(q_slots, permuted, moving, block):
    steps, slots, local, waves = permuted.shape
    cols = moving.shape[2]
    return pl.pallas_call(
        functools.partial(contract_kernel, block),
        out_shape=jax.ShapeDtypeStruct((steps, local, cols), jnp.bfloat16),
        grid_spec=pltpu.PrefetchScalarGridSpec(
            num_scalar_prefetch=1,
            grid=(steps,),
            in_specs=[
                pl.BlockSpec((1, slots, local, waves), lambda i, q: (i, 0, 0, 0)),
                pl.BlockSpec((1, waves, cols), lambda i, q: (i, 0, 0)),
            ],
            out_specs=pl.BlockSpec((1, local, cols), lambda i, q: (i, 0, 0)),
        ),
        cost_estimate=pl.CostEstimate(
            flops=2 * steps * slots * cols * local * waves,
            bytes_accessed=2 * steps * (slots * local * waves + cols * waves + cols * local),
            transcendentals=0,
        ),
    )(q_slots, permuted, moving)


def body(offsets, q_slots, forms, vectors, energies, screened, umklapp):
    kpoint_count = vectors.shape[0]
    vector_count = vectors.shape[1]
    pair_count = vectors.shape[2]
    local_waves = forms.shape[2]
    slot_count = screened.shape[2]
    plane_waves = screened.shape[3]
    step_count = offsets.shape[0]
    ka_size = lax.axis_size("ka")
    ga_size = lax.axis_size("ga")
    ka_bits = ka_size.bit_length() - 1
    ga_bits = ga_size.bit_length() - 1
    me_ka = lax.axis_index("ka")

    projected = lax.dot_general(
        vectors, forms, (((2,), (1,)), ((0,), (0,))), preferred_element_type=jnp.float32
    ).astype(jnp.bfloat16)

    per_piece = slot_count // ka_size
    slab = jnp.transpose(screened[0], (1, 0, 2))
    slab = slab.reshape((2,) * ka_bits + (per_piece, local_waves, plane_waves))
    table = umklapp[0].reshape((2,) * ka_bits + (per_piece, plane_waves))
    roots = [offsets[i] for i in range(step_count)]
    pieces = scatter_from_roots((slab, table), roots, "ka", list(range(ka_bits)))
    waves = jnp.arange(plane_waves, dtype=jnp.int32)
    permuted_pieces = []
    for piece, rows in pieces:
        piece = piece.reshape(per_piece, local_waves, plane_waves)
        rows = rows.reshape(per_piece, plane_waves)
        onehot = (rows[:, :, None] == waves[None, None, :]).astype(jnp.bfloat16)
        moved_cols = lax.dot_general(
            piece, onehot, (((2,), (1,)), ((0,), (0,))), preferred_element_type=jnp.float32
        ).astype(jnp.bfloat16)
        permuted_pieces.append(
            moved_cols.reshape((1,) * ka_bits + (per_piece, local_waves, plane_waves))
        )
    gathered = gather_all(jnp.stack(permuted_pieces), "ka", list(range(ka_bits))[::-1], lead=1)

    moving = [projected] * step_count
    for level in range(ka_bits):
        hopped = from_behind(jnp.stack(moving), "ka", 1 << level)
        moving = [
            jnp.where(roots[i] >> level & 1 == 1, hopped[i], moving[i])
            for i in range(step_count)
        ]
    moving = jnp.stack(moving).reshape(step_count, kpoint_count * vector_count, local_waves)
    moving = jnp.transpose(moving, (0, 2, 1)).reshape(
        (step_count,) + (1,) * ga_bits + (local_waves, kpoint_count * vector_count)
    )
    ga_order = [0, 2, 1] if ga_bits == 3 else list(range(ga_bits))
    moving_all = gather_all(moving, "ga", ga_order, lead=1).reshape(
        step_count, plane_waves, kpoint_count * vector_count
    )

    permuted_all = gathered.reshape(step_count, slot_count, local_waves, plane_waves)
    kernel_part = contract(q_slots, permuted_all, moving_all, vector_count)
    kernel_part = kernel_part.reshape(step_count, local_waves, kpoint_count, vector_count)
    kernel_cat = jnp.concatenate([kernel_part[i] for i in range(step_count)], axis=2)
    action = lax.dot_general(
        kernel_cat, forms, (((0,), (2,)), ((1,), (0,))), preferred_element_type=jnp.float32
    )
    action = action.reshape(kpoint_count, step_count, vector_count, pair_count).sum(axis=1)
    ga_order = [1, 0, 2] if ga_bits == 3 else list(range(ga_bits))
    action = action.reshape((2,) * ga_bits + (kpoint_count // ga_size, vector_count, pair_count))
    action = sum_all(action, "ga", ga_order).reshape(kpoint_count, vector_count, pair_count)
    return energies[:, None, :] * vectors.astype(jnp.float32) - action


def solution(mesh):
    return jax.shard_map(
        body,
        mesh=mesh,
        in_specs=(
            P(),
            P(),
            P("ka", None, "ga"),
            P("ka", None, None),
            P("ka", None),
            P("ka", "ga", None, None),
            P("ka", None, None),
        ),
        out_specs=P("ka", None, None),
        check_vma=False,
    )
```

```python
import functools

import jax
import jax.numpy as jnp
from jax import lax
from jax.experimental import pallas as pl
from jax.experimental.pallas import tpu as pltpu
from jax.sharding import PartitionSpec as P


def from_behind(value, axis, by):
    count = lax.axis_size(axis)
    return lax.ppermute(value, axis, [(i, (i + by) % count) for i in range(count)])


def swap(value, axis, bit):
    count = lax.axis_size(axis)
    return lax.ppermute(value, axis, [(i, i ^ bit) for i in range(count)])


def pick_half(tree, axis_at, which):
    return jax.tree.map(lambda a: lax.dynamic_slice_in_dim(a, which, 1, axis=axis_at), tree)


def scatter_from_roots(own, roots, axis, order):
    nbits = len(order)
    me = lax.axis_index(axis)
    full = (1 << nbits) - 1
    held = [own] * len(roots)
    shared = True
    done_mask = 0
    for bit in order:
        axis_at = nbits - 1 - bit
        mine = (me >> bit) & 1
        if shared:
            sends = pick_half(own, axis_at, 1 - mine)
            got = swap(sends, axis, 1 << bit)
            got = [got] * len(roots)
        else:
            sends = [pick_half(h, axis_at, 1 - mine) for h in held]
            stacked = jax.tree.map(lambda *xs: jnp.stack(xs), *sends)
            stacked = swap(stacked, axis, 1 << bit)
            got = [jax.tree.map(lambda x: x[r], stacked) for r in range(len(roots))]
        new_held = []
        for r, root in enumerate(roots):
            holder = ((me ^ root) & (full & ~done_mask)) == 0
            keep = pick_half(held[r], axis_at, mine)
            new_held.append(
                jax.tree.map(lambda k, g: jnp.where(holder, k, g), keep, got[r])
            )
        held = new_held
        shared = False
        done_mask |= 1 << bit
    return held


def gather_all(pieces, axis, order, lead=0):
    nbits = len(order)
    me = lax.axis_index(axis)
    held = pieces
    for bit in order:
        axis_at = lead + nbits - 1 - bit
        mine = (me >> bit) & 1
        got = swap(held, axis, 1 << bit)

        def join(h, g):
            low = jnp.where(mine == 0, h, g)
            high = jnp.where(mine == 0, g, h)
            return jnp.concatenate([low, high], axis=axis_at)

        held = jax.tree.map(join, held, got)
    return held


def sum_all(value, axis):
    count = lax.axis_size(axis)
    me = lax.axis_index(axis)
    total = lax.dynamic_index_in_dim(value, me, 0, keepdims=False)
    for mask in range(1, count):
        sent = lax.dynamic_index_in_dim(value, me ^ mask, 0, keepdims=False)
        total = total + swap(sent, axis, mask)
    result = jnp.zeros_like(value)
    result = lax.dynamic_update_index_in_dim(result, total, me, 0)
    for mask in range(1, count):
        got = swap(total, axis, mask)
        result = lax.dynamic_update_index_in_dim(result, got, me ^ mask, 0)
    return result


def contract_kernel(block, group, q_ref, perm_ref, mov_ref, out_ref):
    slots, local, waves = perm_ref.shape[1:]

    def some_slots(g, acc):
        first = g * group
        rows = perm_ref[0, pl.ds(first, group)].reshape(group * local, waves)
        product = jnp.dot(rows, mov_ref[0], preferred_element_type=jnp.float32)
        for j in range(group):
            part = product[j * local:(j + 1) * local]
            acc = acc + pltpu.roll(part, q_ref[first + j] * block, 1)
        return acc

    acc = lax.fori_loop(0, slots // group, some_slots, jnp.zeros(out_ref.shape[1:], jnp.float32))
    out_ref[0] = acc.astype(out_ref.dtype)


def contract(q_slots, permuted, moving, block):
    steps, slots, local, waves = permuted.shape
    cols = moving.shape[2]
    return pl.pallas_call(
        functools.partial(contract_kernel, block, 8 if slots % 8 == 0 else 1),
        out_shape=jax.ShapeDtypeStruct((steps, local, cols), jnp.bfloat16),
        grid_spec=pltpu.PrefetchScalarGridSpec(
            num_scalar_prefetch=1,
            grid=(steps,),
            in_specs=[
                pl.BlockSpec((1, slots, local, waves), lambda i, q: (i, 0, 0, 0)),
                pl.BlockSpec((1, waves, cols), lambda i, q: (i, 0, 0)),
            ],
            out_specs=pl.BlockSpec((1, local, cols), lambda i, q: (i, 0, 0)),
        ),
        cost_estimate=pl.CostEstimate(
            flops=2 * steps * slots * cols * local * waves,
            bytes_accessed=2 * steps * (slots * local * waves + cols * waves + cols * local),
            transcendentals=0,
        ),
    )(q_slots, permuted, moving)


def body(offsets, q_slots, forms, vectors, energies, screened, umklapp):
    kpoint_count = vectors.shape[0]
    vector_count = vectors.shape[1]
    pair_count = vectors.shape[2]
    local_waves = forms.shape[2]
    slot_count = screened.shape[2]
    plane_waves = screened.shape[3]
    step_count = offsets.shape[0]
    ka_size = lax.axis_size("ka")
    ga_size = lax.axis_size("ga")
    ka_bits = ka_size.bit_length() - 1
    ga_bits = ga_size.bit_length() - 1
    me_ka = lax.axis_index("ka")

    projected = lax.dot_general(
        vectors, forms, (((2,), (1,)), ((0,), (0,))), preferred_element_type=jnp.float32
    ).astype(jnp.bfloat16)

    per_piece = slot_count // ka_size
    slab = jnp.transpose(screened[0], (1, 0, 2))
    slab = slab.reshape((2,) * ka_bits + (per_piece, local_waves, plane_waves))
    table = umklapp[0].reshape((2,) * ka_bits + (per_piece, plane_waves))
    roots = [offsets[i] for i in range(step_count)]
    pieces = scatter_from_roots((slab, table), roots, "ka", list(range(ka_bits)))
    waves = jnp.arange(plane_waves, dtype=jnp.int32)
    permuted_pieces = []
    for piece, rows in pieces:
        piece = piece.reshape(per_piece, local_waves, plane_waves)
        rows = rows.reshape(per_piece, plane_waves)
        onehot = (rows[:, :, None] == waves[None, None, :]).astype(jnp.bfloat16)
        moved_cols = lax.dot_general(
            piece, onehot, (((2,), (1,)), ((0,), (0,))), preferred_element_type=jnp.float32
        ).astype(jnp.bfloat16)
        permuted_pieces.append(
            moved_cols.reshape((1,) * ka_bits + (per_piece, local_waves, plane_waves))
        )
    gathered = gather_all(jnp.stack(permuted_pieces), "ka", list(range(ka_bits))[::-1], lead=1)

    moving = [projected] * step_count
    for level in range(ka_bits):
        hopped = from_behind(jnp.stack(moving), "ka", 1 << level)
        moving = [
            jnp.where(roots[i] >> level & 1 == 1, hopped[i], moving[i])
            for i in range(step_count)
        ]
    moving = jnp.stack(moving).reshape(step_count, kpoint_count * vector_count, local_waves)
    moving = jnp.transpose(moving, (0, 2, 1)).reshape(
        (step_count,) + (1,) * ga_bits + (local_waves, kpoint_count * vector_count)
    )
    ga_order = [0, 2, 1] if ga_bits == 3 else list(range(ga_bits))
    moving_all = gather_all(moving, "ga", ga_order, lead=1).reshape(
        step_count, plane_waves, kpoint_count * vector_count
    )

    permuted_all = gathered.reshape(step_count, slot_count, local_waves, plane_waves)
    kernel_part = contract(q_slots, permuted_all, moving_all, vector_count)
    kernel_part = kernel_part.reshape(step_count, local_waves, kpoint_count, vector_count)
    kernel_cat = jnp.concatenate([kernel_part[i] for i in range(step_count)], axis=2)
    action = lax.dot_general(
        kernel_cat, forms, (((0,), (2,)), ((1,), (0,))), preferred_element_type=jnp.float32
    )
    action = action.reshape(kpoint_count, step_count, vector_count, pair_count).sum(axis=1)
    action = action.reshape(ga_size, kpoint_count // ga_size, vector_count, pair_count)
    action = sum_all(action, "ga").reshape(kpoint_count, vector_count, pair_count)
    return energies[:, None, :] * vectors.astype(jnp.float32) - action


def solution(mesh):
    return jax.shard_map(
        body,
        mesh=mesh,
        in_specs=(
            P(),
            P(),
            P("ka", None, "ga"),
            P("ka", None, None),
            P("ka", None),
            P("ka", "ga", None, None),
            P("ka", None, None),
        ),
        out_specs=P("ka", None, None),
        check_vma=False,
    )
```

```python
import functools

import jax
import jax.numpy as jnp
from jax import lax
from jax.experimental import pallas as pl
from jax.experimental.pallas import tpu as pltpu
from jax.sharding import PartitionSpec as P


def from_behind(value, axis, by):
    count = lax.axis_size(axis)
    return lax.ppermute(value, axis, [(i, (i + by) % count) for i in range(count)])


def swap(value, axis, bit):
    count = lax.axis_size(axis)
    return lax.ppermute(value, axis, [(i, i ^ bit) for i in range(count)])


def relabel(index, size):
    if size < 8:
        return index
    one = (index >> 1) & 1
    two = (index >> 2) & 1
    swapped = index + (two - one) * 2 + (one - two) * 4
    if isinstance(index, int):
        return swapped if index & 1 else index
    return jnp.where(index & 1 == 1, swapped, index)


def swap_relabelled(value, axis, bit):
    count = lax.axis_size(axis)
    pairs = []
    for i in range(count):
        v = relabel(i, count) ^ (1 << bit)
        pairs.append((i, [j for j in range(count) if relabel(j, count) == v][0]))
    return lax.ppermute(value, axis, pairs)


def pick_half(tree, axis_at, which):
    return jax.tree.map(lambda a: lax.dynamic_slice_in_dim(a, which, 1, axis=axis_at), tree)


def scatter_from_roots(own, roots, axis, order):
    nbits = len(order)
    count = lax.axis_size(axis)
    me = relabel(lax.axis_index(axis), count)
    roots = [relabel(root, count) for root in roots]
    full = (1 << nbits) - 1
    held = [own] * len(roots)
    shared = True
    done_mask = 0
    for bit in order:
        axis_at = nbits - 1 - bit
        mine = (me >> bit) & 1
        if shared:
            sends = pick_half(own, axis_at, 1 - mine)
            got = swap_relabelled(sends, axis, bit)
            got = [got] * len(roots)
        else:
            sends = [pick_half(h, axis_at, 1 - mine) for h in held]
            stacked = jax.tree.map(lambda *xs: jnp.stack(xs), *sends)
            stacked = swap_relabelled(stacked, axis, bit)
            got = [jax.tree.map(lambda x: x[r], stacked) for r in range(len(roots))]
        new_held = []
        for r, root in enumerate(roots):
            holder = ((me ^ root) & (full & ~done_mask)) == 0
            keep = pick_half(held[r], axis_at, mine)
            new_held.append(
                jax.tree.map(lambda k, g: jnp.where(holder, k, g), keep, got[r])
            )
        held = new_held
        shared = False
        done_mask |= 1 << bit
    return held


def gather_all(pieces, axis, order, lead=0, relabelled=False):
    nbits = len(order)
    count = lax.axis_size(axis)
    me = lax.axis_index(axis)
    if relabelled:
        me = relabel(me, count)
    held = pieces
    for bit in order:
        axis_at = lead + nbits - 1 - bit
        mine = (me >> bit) & 1
        if relabelled:
            got = swap_relabelled(held, axis, bit)
        else:
            got = swap(held, axis, 1 << bit)

        def join(h, g):
            low = jnp.where(mine == 0, h, g)
            high = jnp.where(mine == 0, g, h)
            return jnp.concatenate([low, high], axis=axis_at)

        held = jax.tree.map(join, held, got)
    return held


def sum_all(value, axis):
    count = lax.axis_size(axis)
    me = lax.axis_index(axis)
    total = lax.dynamic_index_in_dim(value, me, 0, keepdims=False)
    for mask in range(1, count):
        sent = lax.dynamic_index_in_dim(value, me ^ mask, 0, keepdims=False)
        total = total + swap(sent, axis, mask)
    result = jnp.zeros_like(value)
    result = lax.dynamic_update_index_in_dim(result, total, me, 0)
    for mask in range(1, count):
        got = swap(total, axis, mask)
        result = lax.dynamic_update_index_in_dim(result, got, me ^ mask, 0)
    return result


def contract_kernel(block, group, q_ref, perm_ref, mov_ref, out_ref):
    slots, local, waves = perm_ref.shape[1:]

    def some_slots(g, acc):
        first = g * group
        rows = perm_ref[0, pl.ds(first, group)].reshape(group * local, waves)
        product = jnp.dot(rows, mov_ref[0], preferred_element_type=jnp.float32)
        for j in range(group):
            part = product[j * local:(j + 1) * local]
            acc = acc + pltpu.roll(part, q_ref[first + j] * block, 1)
        return acc

    acc = lax.fori_loop(0, slots // group, some_slots, jnp.zeros(out_ref.shape[1:], jnp.float32))
    out_ref[0] = acc.astype(out_ref.dtype)


def contract(q_slots, permuted, moving, block):
    steps, slots, local, waves = permuted.shape
    cols = moving.shape[2]
    return pl.pallas_call(
        functools.partial(contract_kernel, block, 8 if slots % 8 == 0 else 1),
        out_shape=jax.ShapeDtypeStruct((steps, local, cols), jnp.bfloat16),
        grid_spec=pltpu.PrefetchScalarGridSpec(
            num_scalar_prefetch=1,
            grid=(steps,),
            in_specs=[
                pl.BlockSpec((1, slots, local, waves), lambda i, q: (i, 0, 0, 0)),
                pl.BlockSpec((1, waves, cols), lambda i, q: (i, 0, 0)),
            ],
            out_specs=pl.BlockSpec((1, local, cols), lambda i, q: (i, 0, 0)),
        ),
        cost_estimate=pl.CostEstimate(
            flops=2 * steps * slots * cols * local * waves,
            bytes_accessed=2 * steps * (slots * local * waves + cols * waves + cols * local),
            transcendentals=0,
        ),
    )(q_slots, permuted, moving)


def body(offsets, q_slots, forms, vectors, energies, screened, umklapp):
    kpoint_count = vectors.shape[0]
    vector_count = vectors.shape[1]
    pair_count = vectors.shape[2]
    local_waves = forms.shape[2]
    slot_count = screened.shape[2]
    plane_waves = screened.shape[3]
    step_count = offsets.shape[0]
    ka_size = lax.axis_size("ka")
    ga_size = lax.axis_size("ga")
    ka_bits = ka_size.bit_length() - 1
    ga_bits = ga_size.bit_length() - 1
    me_ka = lax.axis_index("ka")

    projected = lax.dot_general(
        vectors, forms, (((2,), (1,)), ((0,), (0,))), preferred_element_type=jnp.float32
    ).astype(jnp.bfloat16)

    per_piece = slot_count // ka_size
    slab = jnp.transpose(screened[0], (1, 0, 2))
    slab = slab.reshape((2,) * ka_bits + (per_piece, local_waves, plane_waves))
    table = umklapp[0].reshape((2,) * ka_bits + (per_piece, plane_waves))
    roots = [offsets[i] for i in range(step_count)]
    pieces = scatter_from_roots((slab, table), roots, "ka", list(range(ka_bits)))
    waves = jnp.arange(plane_waves, dtype=jnp.int32)
    permuted_pieces = []
    for piece, rows in pieces:
        piece = piece.reshape(per_piece, local_waves, plane_waves)
        rows = rows.reshape(per_piece, plane_waves)
        onehot = (rows[:, :, None] == waves[None, None, :]).astype(jnp.bfloat16)
        moved_cols = lax.dot_general(
            piece, onehot, (((2,), (1,)), ((0,), (0,))), preferred_element_type=jnp.float32
        ).astype(jnp.bfloat16)
        permuted_pieces.append(
            moved_cols.reshape((1,) * ka_bits + (per_piece, local_waves, plane_waves))
        )
    gathered = gather_all(
        jnp.stack(permuted_pieces), "ka", list(range(ka_bits))[::-1], lead=1, relabelled=True
    )

    odd = [roots[i] & 1 for i in range(step_count)]
    hopped = from_behind(projected, "ka", 1)
    moving = [jnp.where(odd[i] == 1, hopped, projected) for i in range(step_count)]
    even_part = [roots[i] - odd[i] for i in range(step_count)]
    amounts = [
        jnp.where(me_ka & 1 == 0, even_part[i], (ka_size - even_part[i]) % ka_size)
        for i in range(step_count)
    ]
    for level in range(1, ka_bits):
        by = 1 << level
        pairs = [
            (j, (j + by) % ka_size if j % 2 == 0 else (j - by) % ka_size) for j in range(ka_size)
        ]
        hopped = lax.ppermute(jnp.stack(moving), "ka", pairs)
        moving = [
            jnp.where(amounts[i] >> level & 1 == 1, hopped[i], moving[i])
            for i in range(step_count)
        ]
    moving = jnp.stack(moving).reshape(step_count, kpoint_count * vector_count, local_waves)
    moving = jnp.transpose(moving, (0, 2, 1)).reshape(
        (step_count,) + (1,) * ga_bits + (local_waves, kpoint_count * vector_count)
    )
    ga_order = [0, 2, 1] if ga_bits == 3 else list(range(ga_bits))
    moving_all = gather_all(moving, "ga", ga_order, lead=1).reshape(
        step_count, plane_waves, kpoint_count * vector_count
    )

    permuted_all = gathered.reshape(step_count, slot_count, local_waves, plane_waves)
    kernel_part = contract(q_slots, permuted_all, moving_all, vector_count)
    kernel_part = kernel_part.reshape(step_count, local_waves, kpoint_count, vector_count)
    kernel_cat = jnp.concatenate([kernel_part[i] for i in range(step_count)], axis=2)
    action = lax.dot_general(
        kernel_cat, forms, (((0,), (2,)), ((1,), (0,))), preferred_element_type=jnp.float32
    )
    action = action.reshape(kpoint_count, step_count, vector_count, pair_count).sum(axis=1)
    action = action.reshape(ga_size, kpoint_count // ga_size, vector_count, pair_count)
    action = sum_all(action, "ga").reshape(kpoint_count, vector_count, pair_count)
    return energies[:, None, :] * vectors.astype(jnp.float32) - action


def solution(mesh):
    return jax.shard_map(
        body,
        mesh=mesh,
        in_specs=(
            P(),
            P(),
            P("ka", None, "ga"),
            P("ka", None, None),
            P("ka", None),
            P("ka", "ga", None, None),
            P("ka", None, None),
        ),
        out_specs=P("ka", None, None),
        check_vma=False,
    )
```

```python
import functools

import jax
import jax.numpy as jnp
from jax import lax
from jax.experimental import pallas as pl
from jax.experimental.pallas import tpu as pltpu
from jax.sharding import PartitionSpec as P


def from_behind(value, axis, by):
    count = lax.axis_size(axis)
    return lax.ppermute(value, axis, [(i, (i + by) % count) for i in range(count)])


def swap(value, axis, bit):
    count = lax.axis_size(axis)
    return lax.ppermute(value, axis, [(i, i ^ bit) for i in range(count)])


def relabel(index, size):
    if size < 8:
        return index
    one = (index >> 1) & 1
    two = (index >> 2) & 1
    swapped = index + (two - one) * 2 + (one - two) * 4
    if isinstance(index, int):
        return swapped if index & 1 else index
    return jnp.where(index & 1 == 1, swapped, index)


def swap_relabelled(value, axis, bit):
    count = lax.axis_size(axis)
    pairs = []
    for i in range(count):
        v = relabel(i, count) ^ (1 << bit)
        pairs.append((i, [j for j in range(count) if relabel(j, count) == v][0]))
    return lax.ppermute(value, axis, pairs)


def pick_half(tree, axis_at, which):
    return jax.tree.map(lambda a: lax.dynamic_slice_in_dim(a, which, 1, axis=axis_at), tree)


def scatter_from_roots(own, roots, axis, order):
    nbits = len(order)
    count = lax.axis_size(axis)
    me = relabel(lax.axis_index(axis), count)
    roots = [relabel(root, count) for root in roots]
    full = (1 << nbits) - 1
    held = [own] * len(roots)
    shared = True
    done_mask = 0
    for bit in order:
        axis_at = nbits - 1 - bit
        mine = (me >> bit) & 1
        if shared:
            sends = pick_half(own, axis_at, 1 - mine)
            got = swap_relabelled(sends, axis, bit)
            got = [got] * len(roots)
        else:
            sends = [pick_half(h, axis_at, 1 - mine) for h in held]
            stacked = jax.tree.map(lambda *xs: jnp.stack(xs), *sends)
            stacked = swap_relabelled(stacked, axis, bit)
            got = [jax.tree.map(lambda x: x[r], stacked) for r in range(len(roots))]
        new_held = []
        for r, root in enumerate(roots):
            holder = ((me ^ root) & (full & ~done_mask)) == 0
            keep = pick_half(held[r], axis_at, mine)
            new_held.append(
                jax.tree.map(lambda k, g: jnp.where(holder, k, g), keep, got[r])
            )
        held = new_held
        shared = False
        done_mask |= 1 << bit
    return held


def gather_all(pieces, axis, order, lead=0, relabelled=False):
    nbits = len(order)
    count = lax.axis_size(axis)
    me = lax.axis_index(axis)
    if relabelled:
        me = relabel(me, count)
    held = pieces
    for bit in order:
        axis_at = lead + nbits - 1 - bit
        mine = (me >> bit) & 1
        if relabelled:
            got = swap_relabelled(held, axis, bit)
        else:
            got = swap(held, axis, 1 << bit)

        def join(h, g):
            low = jnp.where(mine == 0, h, g)
            high = jnp.where(mine == 0, g, h)
            return jnp.concatenate([low, high], axis=axis_at)

        held = jax.tree.map(join, held, got)
    return held


def sum_all(value, axis):
    count = lax.axis_size(axis)
    me = lax.axis_index(axis)
    total = lax.dynamic_index_in_dim(value, me, 0, keepdims=False)
    for mask in range(1, count):
        sent = lax.dynamic_index_in_dim(value, me ^ mask, 0, keepdims=False)
        total = total + swap(sent, axis, mask)
    result = jnp.zeros_like(value)
    result = lax.dynamic_update_index_in_dim(result, total, me, 0)
    for mask in range(1, count):
        got = swap(total, axis, mask)
        result = lax.dynamic_update_index_in_dim(result, got, me ^ mask, 0)
    return result


def gather_flat(value, axis, at):
    count = lax.axis_size(axis)
    me = lax.axis_index(axis)
    shape = value.shape[:at] + (count,) + value.shape[at:]
    result = jnp.zeros(shape, value.dtype)
    result = lax.dynamic_update_index_in_dim(result, value, me, at)
    for mask in range(1, count):
        result = lax.dynamic_update_index_in_dim(result, swap(value, axis, mask), me ^ mask, at)
    return result


def contract_kernel(block, group, q_ref, perm_ref, mov_ref, out_ref):
    slots, local, waves = perm_ref.shape[1:]

    def some_slots(g, acc):
        first = g * group
        rows = perm_ref[0, pl.ds(first, group)].reshape(group * local, waves)
        product = jnp.dot(rows, mov_ref[0], preferred_element_type=jnp.float32)
        for j in range(group):
            part = product[j * local:(j + 1) * local]
            acc = acc + pltpu.roll(part, q_ref[first + j] * block, 1)
        return acc

    acc = lax.fori_loop(0, slots // group, some_slots, jnp.zeros(out_ref.shape[1:], jnp.float32))
    out_ref[0] = acc.astype(out_ref.dtype)


def contract(q_slots, permuted, moving, block):
    steps, slots, local, waves = permuted.shape
    cols = moving.shape[2]
    return pl.pallas_call(
        functools.partial(contract_kernel, block, 8 if slots % 8 == 0 else 1),
        out_shape=jax.ShapeDtypeStruct((steps, local, cols), jnp.bfloat16),
        grid_spec=pltpu.PrefetchScalarGridSpec(
            num_scalar_prefetch=1,
            grid=(steps,),
            in_specs=[
                pl.BlockSpec((1, slots, local, waves), lambda i, q: (i, 0, 0, 0)),
                pl.BlockSpec((1, waves, cols), lambda i, q: (i, 0, 0)),
            ],
            out_specs=pl.BlockSpec((1, local, cols), lambda i, q: (i, 0, 0)),
        ),
        cost_estimate=pl.CostEstimate(
            flops=2 * steps * slots * cols * local * waves,
            bytes_accessed=2 * steps * (slots * local * waves + cols * waves + cols * local),
            transcendentals=0,
        ),
    )(q_slots, permuted, moving)


def body(offsets, q_slots, forms, vectors, energies, screened, umklapp):
    kpoint_count = vectors.shape[0]
    vector_count = vectors.shape[1]
    pair_count = vectors.shape[2]
    local_waves = forms.shape[2]
    slot_count = screened.shape[2]
    plane_waves = screened.shape[3]
    step_count = offsets.shape[0]
    ka_size = lax.axis_size("ka")
    ga_size = lax.axis_size("ga")
    ka_bits = ka_size.bit_length() - 1
    ga_bits = ga_size.bit_length() - 1
    me_ka = lax.axis_index("ka")

    projected = lax.dot_general(
        vectors, forms, (((2,), (1,)), ((0,), (0,))), preferred_element_type=jnp.float32
    ).astype(jnp.bfloat16)

    per_piece = slot_count // ka_size
    slab = jnp.transpose(screened[0], (1, 0, 2))
    slab = slab.reshape((2,) * ka_bits + (per_piece, local_waves, plane_waves))
    table = umklapp[0].reshape((2,) * ka_bits + (per_piece, plane_waves))
    roots = [offsets[i] for i in range(step_count)]
    pieces = scatter_from_roots((slab, table), roots, "ka", list(range(ka_bits)))
    waves = jnp.arange(plane_waves, dtype=jnp.int32)
    permuted_pieces = []
    for piece, rows in pieces:
        piece = piece.reshape(per_piece, local_waves, plane_waves)
        rows = rows.reshape(per_piece, plane_waves)
        onehot = (rows[:, :, None] == waves[None, None, :]).astype(jnp.bfloat16)
        moved_cols = lax.dot_general(
            piece, onehot, (((2,), (1,)), ((0,), (0,))), preferred_element_type=jnp.float32
        ).astype(jnp.bfloat16)
        permuted_pieces.append(
            moved_cols.reshape((1,) * ka_bits + (per_piece, local_waves, plane_waves))
        )
    gathered = gather_all(
        jnp.stack(permuted_pieces), "ka", list(range(ka_bits))[::-1], lead=1, relabelled=True
    )

    odd = [roots[i] & 1 for i in range(step_count)]
    hopped = from_behind(projected, "ka", 1)
    moving = [jnp.where(odd[i] == 1, hopped, projected) for i in range(step_count)]
    even_part = [roots[i] - odd[i] for i in range(step_count)]
    amounts = [
        jnp.where(me_ka & 1 == 0, even_part[i], (ka_size - even_part[i]) % ka_size)
        for i in range(step_count)
    ]
    for level in range(1, ka_bits):
        by = 1 << level
        pairs = [
            (j, (j + by) % ka_size if j % 2 == 0 else (j - by) % ka_size) for j in range(ka_size)
        ]
        hopped = lax.ppermute(jnp.stack(moving), "ka", pairs)
        moving = [
            jnp.where(amounts[i] >> level & 1 == 1, hopped[i], moving[i])
            for i in range(step_count)
        ]
    moving = jnp.stack(moving).reshape(step_count, kpoint_count * vector_count, local_waves)
    moving = jnp.transpose(moving, (0, 2, 1))
    moving_all = gather_flat(moving, "ga", 1).reshape(
        step_count, plane_waves, kpoint_count * vector_count
    )

    permuted_all = gathered.reshape(step_count, slot_count, local_waves, plane_waves)
    kernel_part = contract(q_slots, permuted_all, moving_all, vector_count)
    kernel_part = kernel_part.reshape(step_count, local_waves, kpoint_count, vector_count)
    kernel_cat = jnp.concatenate([kernel_part[i] for i in range(step_count)], axis=2)
    action = lax.dot_general(
        kernel_cat, forms, (((0,), (2,)), ((1,), (0,))), preferred_element_type=jnp.float32
    )
    action = action.reshape(kpoint_count, step_count, vector_count, pair_count).sum(axis=1)
    action = action.reshape(ga_size, kpoint_count // ga_size, vector_count, pair_count)
    action = sum_all(action, "ga").reshape(kpoint_count, vector_count, pair_count)
    return energies[:, None, :] * vectors.astype(jnp.float32) - action


def solution(mesh):
    return jax.shard_map(
        body,
        mesh=mesh,
        in_specs=(
            P(),
            P(),
            P("ka", None, "ga"),
            P("ka", None, None),
            P("ka", None),
            P("ka", "ga", None, None),
            P("ka", None, None),
        ),
        out_specs=P("ka", None, None),
        check_vma=False,
    )
```

```python
import functools

import jax
import jax.numpy as jnp
from jax import lax
from jax.experimental import pallas as pl
from jax.experimental.pallas import tpu as pltpu
from jax.sharding import PartitionSpec as P


def from_behind(value, axis, by):
    count = lax.axis_size(axis)
    return lax.ppermute(value, axis, [(i, (i + by) % count) for i in range(count)])


def swap(value, axis, bit):
    count = lax.axis_size(axis)
    return lax.ppermute(value, axis, [(i, i ^ bit) for i in range(count)])


def relabel(index, size):
    if size < 8:
        return index
    one = (index >> 1) & 1
    two = (index >> 2) & 1
    swapped = index + (two - one) * 2 + (one - two) * 4
    if isinstance(index, int):
        return swapped if index & 1 else index
    return jnp.where(index & 1 == 1, swapped, index)


def swap_relabelled(value, axis, bit):
    count = lax.axis_size(axis)
    pairs = []
    for i in range(count):
        v = relabel(i, count) ^ (1 << bit)
        pairs.append((i, [j for j in range(count) if relabel(j, count) == v][0]))
    return lax.ppermute(value, axis, pairs)


def lockstep(chains):
    states = [next(chain) for chain in chains]
    results = [None] * len(chains)
    live = list(range(len(chains)))
    while live:
        tied = lax.optimization_barrier([states[i] for i in live])
        still = []
        for i, state in zip(live, tied):
            try:
                states[i] = chains[i].send(state)
                still.append(i)
            except StopIteration as stop:
                results[i] = stop.value
        live = still
    return results


def pick_half(tree, axis_at, which):
    return jax.tree.map(lambda a: lax.dynamic_slice_in_dim(a, which, 1, axis=axis_at), tree)


def scatter_rounds(own, roots, axis, order):
    nbits = len(order)
    count = lax.axis_size(axis)
    me = relabel(lax.axis_index(axis), count)
    roots = [relabel(root, count) for root in roots]
    full = (1 << nbits) - 1
    held = [own] * len(roots)
    shared = True
    done_mask = 0
    for bit in order:
        axis_at = nbits - 1 - bit
        mine = (me >> bit) & 1
        if shared:
            sends = pick_half(own, axis_at, 1 - mine)
            got = swap_relabelled(sends, axis, bit)
            got = [got] * len(roots)
        else:
            sends = [pick_half(h, axis_at, 1 - mine) for h in held]
            stacked = jax.tree.map(lambda *xs: jnp.stack(xs), *sends)
            stacked = swap_relabelled(stacked, axis, bit)
            got = [jax.tree.map(lambda x: x[r], stacked) for r in range(len(roots))]
        new_held = []
        for r, root in enumerate(roots):
            holder = ((me ^ root) & (full & ~done_mask)) == 0
            keep = pick_half(held[r], axis_at, mine)
            new_held.append(
                jax.tree.map(lambda k, g: jnp.where(holder, k, g), keep, got[r])
            )
        held = yield new_held
        shared = False
        done_mask |= 1 << bit
    return held


def gather_rounds(pieces, axis, order, lead=0, relabelled=False):
    nbits = len(order)
    count = lax.axis_size(axis)
    me = lax.axis_index(axis)
    if relabelled:
        me = relabel(me, count)
    held = pieces
    for bit in order:
        axis_at = lead + nbits - 1 - bit
        mine = (me >> bit) & 1
        if relabelled:
            got = swap_relabelled(held, axis, bit)
        else:
            got = swap(held, axis, 1 << bit)

        def join(h, g):
            low = jnp.where(mine == 0, h, g)
            high = jnp.where(mine == 0, g, h)
            return jnp.concatenate([low, high], axis=axis_at)

        held = yield jax.tree.map(join, held, got)
    return held


def sum_all(value, axis):
    count = lax.axis_size(axis)
    me = lax.axis_index(axis)
    total = lax.dynamic_index_in_dim(value, me, 0, keepdims=False)
    for mask in range(1, count):
        sent = lax.dynamic_index_in_dim(value, me ^ mask, 0, keepdims=False)
        total = total + swap(sent, axis, mask)
    result = jnp.zeros_like(value)
    result = lax.dynamic_update_index_in_dim(result, total, me, 0)
    for mask in range(1, count):
        got = swap(total, axis, mask)
        result = lax.dynamic_update_index_in_dim(result, got, me ^ mask, 0)
    return result


def contract_kernel(block, group, q_ref, perm_ref, mov_ref, out_ref):
    slots, local, waves = perm_ref.shape[1:]

    def some_slots(g, acc):
        first = g * group
        rows = perm_ref[0, pl.ds(first, group)].reshape(group * local, waves)
        product = jnp.dot(rows, mov_ref[0], preferred_element_type=jnp.float32)
        for j in range(group):
            part = product[j * local:(j + 1) * local]
            acc = acc + pltpu.roll(part, q_ref[first + j] * block, 1)
        return acc

    acc = lax.fori_loop(0, slots // group, some_slots, jnp.zeros(out_ref.shape[1:], jnp.float32))
    out_ref[0] = acc.astype(out_ref.dtype)


def contract(q_slots, permuted, moving, block):
    steps, slots, local, waves = permuted.shape
    cols = moving.shape[2]
    return pl.pallas_call(
        functools.partial(contract_kernel, block, 8 if slots % 8 == 0 else 1),
        out_shape=jax.ShapeDtypeStruct((steps, local, cols), jnp.bfloat16),
        grid_spec=pltpu.PrefetchScalarGridSpec(
            num_scalar_prefetch=1,
            grid=(steps,),
            in_specs=[
                pl.BlockSpec((1, slots, local, waves), lambda i, q: (i, 0, 0, 0)),
                pl.BlockSpec((1, waves, cols), lambda i, q: (i, 0, 0)),
            ],
            out_specs=pl.BlockSpec((1, local, cols), lambda i, q: (i, 0, 0)),
        ),
        cost_estimate=pl.CostEstimate(
            flops=2 * steps * slots * cols * local * waves,
            bytes_accessed=2 * steps * (slots * local * waves + cols * waves + cols * local),
            transcendentals=0,
        ),
    )(q_slots, permuted, moving)


def body(offsets, q_slots, forms, vectors, energies, screened, umklapp):
    kpoint_count = vectors.shape[0]
    vector_count = vectors.shape[1]
    pair_count = vectors.shape[2]
    local_waves = forms.shape[2]
    slot_count = screened.shape[2]
    plane_waves = screened.shape[3]
    step_count = offsets.shape[0]
    ka_size = lax.axis_size("ka")
    ga_size = lax.axis_size("ga")
    ka_bits = ka_size.bit_length() - 1
    ga_bits = ga_size.bit_length() - 1
    me_ka = lax.axis_index("ka")

    projected = lax.dot_general(
        vectors, forms, (((2,), (1,)), ((0,), (0,))), preferred_element_type=jnp.float32
    ).astype(jnp.bfloat16)

    per_piece = slot_count // ka_size
    slab = jnp.transpose(screened[0], (1, 0, 2))
    slab = slab.reshape((2,) * ka_bits + (per_piece, local_waves, plane_waves))
    table = umklapp[0].reshape((2,) * ka_bits + (per_piece, plane_waves))
    roots = [offsets[i] for i in range(step_count)]
    waves = jnp.arange(plane_waves, dtype=jnp.int32)

    def broadcast_chain():
        pieces = yield from scatter_rounds((slab, table), roots, "ka", list(range(ka_bits)))
        permuted_pieces = []
        for piece, rows in pieces:
            piece = piece.reshape(per_piece, local_waves, plane_waves)
            rows = rows.reshape(per_piece, plane_waves)
            onehot = (rows[:, :, None] == waves[None, None, :]).astype(jnp.bfloat16)
            moved_cols = lax.dot_general(
                piece, onehot, (((2,), (1,)), ((0,), (0,))), preferred_element_type=jnp.float32
            ).astype(jnp.bfloat16)
            permuted_pieces.append(
                moved_cols.reshape((1,) * ka_bits + (per_piece, local_waves, plane_waves))
            )
        gathered = yield from gather_rounds(
            jnp.stack(permuted_pieces), "ka", list(range(ka_bits))[::-1], lead=1, relabelled=True
        )
        return gathered

    def roll_chain():
        odd = [roots[i] & 1 for i in range(step_count)]
        hopped = from_behind(projected, "ka", 1)
        moving = [jnp.where(odd[i] == 1, hopped, projected) for i in range(step_count)]
        moving = yield moving
        even_part = [roots[i] - odd[i] for i in range(step_count)]
        amounts = [
            jnp.where(me_ka & 1 == 0, even_part[i], (ka_size - even_part[i]) % ka_size)
            for i in range(step_count)
        ]
        for level in range(1, ka_bits):
            by = 1 << level
            pairs = [
                (j, (j + by) % ka_size if j % 2 == 0 else (j - by) % ka_size)
                for j in range(ka_size)
            ]
            hopped = lax.ppermute(jnp.stack(moving), "ka", pairs)
            moving = [
                jnp.where(amounts[i] >> level & 1 == 1, hopped[i], moving[i])
                for i in range(step_count)
            ]
            moving = yield moving
        moving = jnp.stack(moving).reshape(step_count, kpoint_count * vector_count, local_waves)
        moving = jnp.transpose(moving, (0, 2, 1)).reshape(
            (step_count,) + (1,) * ga_bits + (local_waves, kpoint_count * vector_count)
        )
        ga_order = [0, 2, 1] if ga_bits == 3 else list(range(ga_bits))
        moving_all = yield from gather_rounds(moving, "ga", ga_order, lead=1)
        return moving_all.reshape(step_count, plane_waves, kpoint_count * vector_count)

    gathered, moving_all = lockstep([broadcast_chain(), roll_chain()])

    permuted_all = gathered.reshape(step_count, slot_count, local_waves, plane_waves)
    kernel_part = contract(q_slots, permuted_all, moving_all, vector_count)
    kernel_part = kernel_part.reshape(step_count, local_waves, kpoint_count, vector_count)
    kernel_cat = jnp.concatenate([kernel_part[i] for i in range(step_count)], axis=2)
    action = lax.dot_general(
        kernel_cat, forms, (((0,), (2,)), ((1,), (0,))), preferred_element_type=jnp.float32
    )
    action = action.reshape(kpoint_count, step_count, vector_count, pair_count).sum(axis=1)
    action = action.reshape(ga_size, kpoint_count // ga_size, vector_count, pair_count)
    action = sum_all(action, "ga").reshape(kpoint_count, vector_count, pair_count)
    return energies[:, None, :] * vectors.astype(jnp.float32) - action


def solution(mesh):
    return jax.shard_map(
        body,
        mesh=mesh,
        in_specs=(
            P(),
            P(),
            P("ka", None, "ga"),
            P("ka", None, None),
            P("ka", None),
            P("ka", "ga", None, None),
            P("ka", None, None),
        ),
        out_specs=P("ka", None, None),
        check_vma=False,
    )
```

```python
import functools

import jax
import jax.numpy as jnp
from jax import lax
from jax.experimental import pallas as pl
from jax.experimental.pallas import tpu as pltpu
from jax.sharding import PartitionSpec as P


def from_behind(value, axis, by):
    count = lax.axis_size(axis)
    return lax.ppermute(value, axis, [(i, (i + by) % count) for i in range(count)])


def swap(value, axis, bit):
    count = lax.axis_size(axis)
    return lax.ppermute(value, axis, [(i, i ^ bit) for i in range(count)])


def relabel(index, size):
    if size < 8:
        return index
    one = (index >> 1) & 1
    two = (index >> 2) & 1
    swapped = index + (two - one) * 2 + (one - two) * 4
    if isinstance(index, int):
        return swapped if index & 1 else index
    return jnp.where(index & 1 == 1, swapped, index)


def swap_relabelled(value, axis, bit):
    count = lax.axis_size(axis)
    pairs = []
    for i in range(count):
        v = relabel(i, count) ^ (1 << bit)
        pairs.append((i, [j for j in range(count) if relabel(j, count) == v][0]))
    return lax.ppermute(value, axis, pairs)


def pick_half(tree, axis_at, which):
    return jax.tree.map(lambda a: lax.dynamic_slice_in_dim(a, which, 1, axis=axis_at), tree)


def scatter_from_roots(own, roots, axis, order):
    nbits = len(order)
    count = lax.axis_size(axis)
    me = relabel(lax.axis_index(axis), count)
    roots = [relabel(root, count) for root in roots]
    full = (1 << nbits) - 1
    held = [own] * len(roots)
    shared = True
    done_mask = 0
    for bit in order:
        axis_at = nbits - 1 - bit
        mine = (me >> bit) & 1
        if shared:
            sends = pick_half(own, axis_at, 1 - mine)
            got = swap_relabelled(sends, axis, bit)
            got = [got] * len(roots)
        else:
            sends = [pick_half(h, axis_at, 1 - mine) for h in held]
            stacked = jax.tree.map(lambda *xs: jnp.stack(xs), *sends)
            stacked = swap_relabelled(stacked, axis, bit)
            got = [jax.tree.map(lambda x: x[r], stacked) for r in range(len(roots))]
        new_held = []
        for r, root in enumerate(roots):
            holder = ((me ^ root) & (full & ~done_mask)) == 0
            keep = pick_half(held[r], axis_at, mine)
            new_held.append(
                jax.tree.map(lambda k, g: jnp.where(holder, k, g), keep, got[r])
            )
        held = new_held
        shared = False
        done_mask |= 1 << bit
    return held


def gather_all(pieces, axis, order, lead=0, relabelled=False):
    nbits = len(order)
    count = lax.axis_size(axis)
    me = lax.axis_index(axis)
    if relabelled:
        me = relabel(me, count)
    held = pieces
    for bit in order:
        axis_at = lead + nbits - 1 - bit
        mine = (me >> bit) & 1
        if relabelled:
            got = swap_relabelled(held, axis, bit)
        else:
            got = swap(held, axis, 1 << bit)

        def join(h, g):
            low = jnp.where(mine == 0, h, g)
            high = jnp.where(mine == 0, g, h)
            return jnp.concatenate([low, high], axis=axis_at)

        held = jax.tree.map(join, held, got)
    return held


def sum_all(value, axis):
    count = lax.axis_size(axis)
    me = lax.axis_index(axis)
    total = lax.dynamic_index_in_dim(value, me, 0, keepdims=False)
    for mask in range(1, count):
        sent = lax.dynamic_index_in_dim(value, me ^ mask, 0, keepdims=False)
        total = total + swap(sent, axis, mask)
    result = jnp.zeros_like(value)
    result = lax.dynamic_update_index_in_dim(result, total, me, 0)
    for mask in range(1, count):
        got = swap(total, axis, mask)
        result = lax.dynamic_update_index_in_dim(result, got, me ^ mask, 0)
    return result


def contract_kernel(block, group, q_ref, perm_ref, mov_ref, out_ref):
    slots, local, waves = perm_ref.shape[1:]

    def some_slots(g, acc):
        first = g * group
        rows = perm_ref[0, pl.ds(first, group)].reshape(group * local, waves)
        product = jnp.dot(rows, mov_ref[0], preferred_element_type=jnp.float32)
        for j in range(group):
            part = product[j * local:(j + 1) * local]
            acc = acc + pltpu.roll(part, q_ref[first + j] * block, 1)
        return acc

    acc = lax.fori_loop(0, slots // group, some_slots, jnp.zeros(out_ref.shape[1:], jnp.float32))
    out_ref[0] = acc.astype(out_ref.dtype)


def contract(q_slots, permuted, moving, block):
    steps, slots, local, waves = permuted.shape
    cols = moving.shape[2]
    return pl.pallas_call(
        functools.partial(contract_kernel, block, 8 if slots % 8 == 0 else 1),
        out_shape=jax.ShapeDtypeStruct((steps, local, cols), jnp.bfloat16),
        grid_spec=pltpu.PrefetchScalarGridSpec(
            num_scalar_prefetch=1,
            grid=(steps,),
            in_specs=[
                pl.BlockSpec((1, slots, local, waves), lambda i, q: (i, 0, 0, 0)),
                pl.BlockSpec((1, waves, cols), lambda i, q: (i, 0, 0)),
            ],
            out_specs=pl.BlockSpec((1, local, cols), lambda i, q: (i, 0, 0)),
        ),
        cost_estimate=pl.CostEstimate(
            flops=2 * steps * slots * cols * local * waves,
            bytes_accessed=2 * steps * (slots * local * waves + cols * waves + cols * local),
            transcendentals=0,
        ),
    )(q_slots, permuted, moving)


def body(offsets, q_slots, forms, vectors, energies, screened, umklapp):
    kpoint_count = vectors.shape[0]
    vector_count = vectors.shape[1]
    pair_count = vectors.shape[2]
    local_waves = forms.shape[2]
    slot_count = screened.shape[2]
    plane_waves = screened.shape[3]
    step_count = offsets.shape[0]
    ka_size = lax.axis_size("ka")
    ga_size = lax.axis_size("ga")
    ka_bits = ka_size.bit_length() - 1
    ga_bits = ga_size.bit_length() - 1
    me_ka = lax.axis_index("ka")

    projected = lax.dot_general(
        vectors, forms, (((2,), (1,)), ((0,), (0,))), preferred_element_type=jnp.float32
    ).astype(jnp.bfloat16)

    per_piece = slot_count // ka_size
    slab = jnp.transpose(screened[0], (1, 0, 2))
    table = (umklapp[0] - plane_waves // 2).astype(jnp.bfloat16)[:, None, :]
    slab = jnp.concatenate([slab, table], axis=1)
    slab = slab.reshape((2,) * ka_bits + (per_piece, local_waves + 1, plane_waves))
    roots = [offsets[i] for i in range(step_count)]
    pieces = scatter_from_roots(slab, roots, "ka", list(range(ka_bits)))
    waves = jnp.arange(plane_waves, dtype=jnp.int32)
    permuted_pieces = []
    for piece in pieces:
        piece = piece.reshape(per_piece, local_waves + 1, plane_waves)
        rows = piece[:, local_waves, :].astype(jnp.int32) + plane_waves // 2
        piece = piece[:, :local_waves, :]
        onehot = (rows[:, :, None] == waves[None, None, :]).astype(jnp.bfloat16)
        moved_cols = lax.dot_general(
            piece, onehot, (((2,), (1,)), ((0,), (0,))), preferred_element_type=jnp.float32
        ).astype(jnp.bfloat16)
        permuted_pieces.append(
            moved_cols.reshape((1,) * ka_bits + (per_piece, local_waves, plane_waves))
        )
    gathered = gather_all(
        jnp.stack(permuted_pieces), "ka", list(range(ka_bits))[::-1], lead=1, relabelled=True
    )

    odd = [roots[i] & 1 for i in range(step_count)]
    hopped = from_behind(projected, "ka", 1)
    moving = [jnp.where(odd[i] == 1, hopped, projected) for i in range(step_count)]
    even_part = [roots[i] - odd[i] for i in range(step_count)]
    amounts = [
        jnp.where(me_ka & 1 == 0, even_part[i], (ka_size - even_part[i]) % ka_size)
        for i in range(step_count)
    ]
    for level in range(1, ka_bits):
        by = 1 << level
        pairs = [
            (j, (j + by) % ka_size if j % 2 == 0 else (j - by) % ka_size) for j in range(ka_size)
        ]
        hopped = lax.ppermute(jnp.stack(moving), "ka", pairs)
        moving = [
            jnp.where(amounts[i] >> level & 1 == 1, hopped[i], moving[i])
            for i in range(step_count)
        ]
    moving = jnp.stack(moving).reshape(step_count, kpoint_count * vector_count, local_waves)
    moving = jnp.transpose(moving, (0, 2, 1)).reshape(
        (step_count,) + (1,) * ga_bits + (local_waves, kpoint_count * vector_count)
    )
    ga_order = [0, 2, 1] if ga_bits == 3 else list(range(ga_bits))
    moving_all = gather_all(moving, "ga", ga_order, lead=1).reshape(
        step_count, plane_waves, kpoint_count * vector_count
    )

    permuted_all = gathered.reshape(step_count, slot_count, local_waves, plane_waves)
    kernel_part = contract(q_slots, permuted_all, moving_all, vector_count)
    kernel_part = kernel_part.reshape(step_count, local_waves, kpoint_count, vector_count)
    kernel_cat = jnp.concatenate([kernel_part[i] for i in range(step_count)], axis=2)
    action = lax.dot_general(
        kernel_cat, forms, (((0,), (2,)), ((1,), (0,))), preferred_element_type=jnp.float32
    )
    action = action.reshape(kpoint_count, step_count, vector_count, pair_count).sum(axis=1)
    action = action.reshape(ga_size, kpoint_count // ga_size, vector_count, pair_count)
    action = sum_all(action, "ga").reshape(kpoint_count, vector_count, pair_count)
    return energies[:, None, :] * vectors.astype(jnp.float32) - action


def solution(mesh):
    return jax.shard_map(
        body,
        mesh=mesh,
        in_specs=(
            P(),
            P(),
            P("ka", None, "ga"),
            P("ka", None, None),
            P("ka", None),
            P("ka", "ga", None, None),
            P("ka", None, None),
        ),
        out_specs=P("ka", None, None),
        check_vma=False,
    )
```

```python
import functools

import jax
import jax.numpy as jnp
from jax import lax
from jax.experimental import pallas as pl
from jax.experimental.pallas import tpu as pltpu
from jax.sharding import PartitionSpec as P


def from_behind(value, axis, by):
    count = lax.axis_size(axis)
    return lax.ppermute(value, axis, [(i, (i + by) % count) for i in range(count)])


def swap(value, axis, bit):
    count = lax.axis_size(axis)
    return lax.ppermute(value, axis, [(i, i ^ bit) for i in range(count)])


def relabel(index, size):
    if size < 8:
        return index
    one = (index >> 1) & 1
    two = (index >> 2) & 1
    swapped = index + (two - one) * 2 + (one - two) * 4
    if isinstance(index, int):
        return swapped if index & 1 else index
    return jnp.where(index & 1 == 1, swapped, index)


def swap_relabelled(value, axis, bit):
    count = lax.axis_size(axis)
    pairs = []
    for i in range(count):
        v = relabel(i, count) ^ (1 << bit)
        pairs.append((i, [j for j in range(count) if relabel(j, count) == v][0]))
    return lax.ppermute(value, axis, pairs)


def pick_half(tree, axis_at, which):
    return jax.tree.map(lambda a: lax.dynamic_slice_in_dim(a, which, 1, axis=axis_at), tree)


def scatter_from_roots(own, roots, axis, order):
    nbits = len(order)
    count = lax.axis_size(axis)
    me = relabel(lax.axis_index(axis), count)
    roots = [relabel(root, count) for root in roots]
    full = (1 << nbits) - 1
    held = [own] * len(roots)
    shared = True
    done_mask = 0
    for bit in order:
        axis_at = nbits - 1 - bit
        mine = (me >> bit) & 1
        if shared:
            sends = pick_half(own, axis_at, 1 - mine)
            got = swap_relabelled(sends, axis, bit)
            got = [got] * len(roots)
        else:
            sends = [pick_half(h, axis_at, 1 - mine) for h in held]
            stacked = jax.tree.map(lambda *xs: jnp.stack(xs), *sends)
            stacked = swap_relabelled(stacked, axis, bit)
            got = [jax.tree.map(lambda x: x[r], stacked) for r in range(len(roots))]
        new_held = []
        for r, root in enumerate(roots):
            holder = ((me ^ root) & (full & ~done_mask)) == 0
            keep = pick_half(held[r], axis_at, mine)
            new_held.append(
                jax.tree.map(lambda k, g: jnp.where(holder, k, g), keep, got[r])
            )
        held = new_held
        shared = False
        done_mask |= 1 << bit
    return held


def gather_all(pieces, axis, order, lead=0, relabelled=False):
    nbits = len(order)
    count = lax.axis_size(axis)
    me = lax.axis_index(axis)
    if relabelled:
        me = relabel(me, count)
    held = pieces
    for bit in order:
        axis_at = lead + nbits - 1 - bit
        mine = (me >> bit) & 1
        if relabelled:
            got = swap_relabelled(held, axis, bit)
        else:
            got = swap(held, axis, 1 << bit)

        def join(h, g):
            low = jnp.where(mine == 0, h, g)
            high = jnp.where(mine == 0, g, h)
            return jnp.concatenate([low, high], axis=axis_at)

        held = jax.tree.map(join, held, got)
    return held


def sum_all(value, axis, order):
    nbits = len(order)
    me = lax.axis_index(axis)
    held = value
    for bit in order:
        axis_at = nbits - 1 - bit
        mine = (me >> bit) & 1
        sends = lax.dynamic_slice_in_dim(held, 1 - mine, 1, axis=axis_at)
        keep = lax.dynamic_slice_in_dim(held, mine, 1, axis=axis_at)
        held = keep + swap(sends, axis, 1 << bit)
    return gather_all(held, axis, order[::-1])


def contract_kernel(block, group, q_ref, perm_ref, mov_ref, out_ref):
    slots, local, waves = perm_ref.shape[1:]

    def some_slots(g, acc):
        first = g * group
        rows = perm_ref[0, pl.ds(first, group)].reshape(group * local, waves)
        product = jnp.dot(rows, mov_ref[0], preferred_element_type=jnp.float32)
        for j in range(group):
            part = product[j * local:(j + 1) * local]
            acc = acc + pltpu.roll(part, q_ref[first + j] * block, 1)
        return acc

    acc = lax.fori_loop(0, slots // group, some_slots, jnp.zeros(out_ref.shape[1:], jnp.float32))
    out_ref[0] = acc.astype(out_ref.dtype)


def contract(q_slots, permuted, moving, block):
    steps, slots, local, waves = permuted.shape
    cols = moving.shape[2]
    return pl.pallas_call(
        functools.partial(contract_kernel, block, 8 if slots % 8 == 0 else 1),
        out_shape=jax.ShapeDtypeStruct((steps, local, cols), jnp.bfloat16),
        grid_spec=pltpu.PrefetchScalarGridSpec(
            num_scalar_prefetch=1,
            grid=(steps,),
            in_specs=[
                pl.BlockSpec((1, slots, local, waves), lambda i, q: (i, 0, 0, 0)),
                pl.BlockSpec((1, waves, cols), lambda i, q: (i, 0, 0)),
            ],
            out_specs=pl.BlockSpec((1, local, cols), lambda i, q: (i, 0, 0)),
        ),
        cost_estimate=pl.CostEstimate(
            flops=2 * steps * slots * cols * local * waves,
            bytes_accessed=2 * steps * (slots * local * waves + cols * waves + cols * local),
            transcendentals=0,
        ),
    )(q_slots, permuted, moving)


def body(offsets, q_slots, forms, vectors, energies, screened, umklapp):
    kpoint_count = vectors.shape[0]
    vector_count = vectors.shape[1]
    pair_count = vectors.shape[2]
    local_waves = forms.shape[2]
    slot_count = screened.shape[2]
    plane_waves = screened.shape[3]
    step_count = offsets.shape[0]
    ka_size = lax.axis_size("ka")
    ga_size = lax.axis_size("ga")
    ka_bits = ka_size.bit_length() - 1
    ga_bits = ga_size.bit_length() - 1
    me_ka = lax.axis_index("ka")

    projected = lax.dot_general(
        vectors, forms, (((2,), (1,)), ((0,), (0,))), preferred_element_type=jnp.float32
    ).astype(jnp.bfloat16)

    per_piece = slot_count // ka_size
    slab = jnp.transpose(screened[0], (1, 0, 2))
    slab = slab.reshape((2,) * ka_bits + (per_piece, local_waves, plane_waves))
    table = umklapp[0].reshape((2,) * ka_bits + (per_piece, plane_waves))
    roots = [offsets[i] for i in range(step_count)]
    pieces = scatter_from_roots((slab, table), roots, "ka", list(range(ka_bits)))
    waves = jnp.arange(plane_waves, dtype=jnp.int32)
    permuted_pieces = []
    for piece, rows in pieces:
        piece = piece.reshape(per_piece, local_waves, plane_waves)
        rows = rows.reshape(per_piece, plane_waves)
        onehot = (rows[:, :, None] == waves[None, None, :]).astype(jnp.bfloat16)
        moved_cols = lax.dot_general(
            piece, onehot, (((2,), (1,)), ((0,), (0,))), preferred_element_type=jnp.float32
        ).astype(jnp.bfloat16)
        permuted_pieces.append(
            moved_cols.reshape((1,) * ka_bits + (per_piece, local_waves, plane_waves))
        )
    gathered = gather_all(
        jnp.stack(permuted_pieces), "ka", list(range(ka_bits))[::-1], lead=1, relabelled=True
    )

    odd = [roots[i] & 1 for i in range(step_count)]
    hopped = from_behind(projected, "ka", 1)
    moving = [jnp.where(odd[i] == 1, hopped, projected) for i in range(step_count)]
    even_part = [roots[i] - odd[i] for i in range(step_count)]
    amounts = [
        jnp.where(me_ka & 1 == 0, even_part[i], (ka_size - even_part[i]) % ka_size)
        for i in range(step_count)
    ]
    for level in range(1, ka_bits):
        by = 1 << level
        pairs = [
            (j, (j + by) % ka_size if j % 2 == 0 else (j - by) % ka_size) for j in range(ka_size)
        ]
        hopped = lax.ppermute(jnp.stack(moving), "ka", pairs)
        moving = [
            jnp.where(amounts[i] >> level & 1 == 1, hopped[i], moving[i])
            for i in range(step_count)
        ]
    moving = jnp.stack(moving).reshape(step_count, kpoint_count * vector_count, local_waves)
    moving = jnp.transpose(moving, (0, 2, 1)).reshape(
        (step_count,) + (1,) * ga_bits + (local_waves, kpoint_count * vector_count)
    )
    ga_order = [0, 2, 1] if ga_bits == 3 else list(range(ga_bits))
    moving_all = gather_all(moving, "ga", ga_order, lead=1).reshape(
        step_count, plane_waves, kpoint_count * vector_count
    )

    permuted_all = gathered.reshape(step_count, slot_count, local_waves, plane_waves)
    kernel_part = contract(q_slots, permuted_all, moving_all, vector_count)
    kernel_part = kernel_part.reshape(step_count, local_waves, kpoint_count, vector_count)
    kernel_cat = jnp.concatenate([kernel_part[i] for i in range(step_count)], axis=2)
    action = lax.dot_general(
        kernel_cat, forms, (((0,), (2,)), ((1,), (0,))), preferred_element_type=jnp.float32
    )
    action = action.reshape(kpoint_count, step_count, vector_count, pair_count).sum(axis=1)
    sum_order = [1, 0, 2] if ga_bits == 3 else list(range(ga_bits))
    action = action.reshape((2,) * ga_bits + (kpoint_count // ga_size, vector_count, pair_count))
    action = sum_all(action, "ga", sum_order).reshape(kpoint_count, vector_count, pair_count)
    return energies[:, None, :] * vectors.astype(jnp.float32) - action


def solution(mesh):
    return jax.shard_map(
        body,
        mesh=mesh,
        in_specs=(
            P(),
            P(),
            P("ka", None, "ga"),
            P("ka", None, None),
            P("ka", None),
            P("ka", "ga", None, None),
            P("ka", None, None),
        ),
        out_specs=P("ka", None, None),
        check_vma=False,
    )
```

```python
import functools

import jax
import jax.numpy as jnp
from jax import lax
from jax.experimental import pallas as pl
from jax.experimental.pallas import tpu as pltpu
from jax.sharding import PartitionSpec as P


def from_behind(value, axis, by):
    count = lax.axis_size(axis)
    return lax.ppermute(value, axis, [(i, (i + by) % count) for i in range(count)])


def swap(value, axis, bit):
    count = lax.axis_size(axis)
    return lax.ppermute(value, axis, [(i, i ^ bit) for i in range(count)])


def relabel(index, size):
    if size < 8:
        return index
    one = (index >> 1) & 1
    two = (index >> 2) & 1
    swapped = index + (two - one) * 2 + (one - two) * 4
    if isinstance(index, int):
        return swapped if index & 1 else index
    return jnp.where(index & 1 == 1, swapped, index)


def swap_relabelled(value, axis, bit):
    count = lax.axis_size(axis)
    pairs = []
    for i in range(count):
        v = relabel(i, count) ^ (1 << bit)
        pairs.append((i, [j for j in range(count) if relabel(j, count) == v][0]))
    return lax.ppermute(value, axis, pairs)


def pick_half(tree, axis_at, which):
    return jax.tree.map(lambda a: lax.dynamic_slice_in_dim(a, which, 1, axis=axis_at), tree)


def scatter_from_roots(own, roots, axis, order):
    nbits = len(order)
    count = lax.axis_size(axis)
    me = relabel(lax.axis_index(axis), count)
    roots = [relabel(root, count) for root in roots]
    full = (1 << nbits) - 1
    held = [own] * len(roots)
    shared = True
    done_mask = 0
    for bit in order:
        axis_at = nbits - 1 - bit
        mine = (me >> bit) & 1
        if shared:
            sends = pick_half(own, axis_at, 1 - mine)
            got = swap_relabelled(sends, axis, bit)
            got = [got] * len(roots)
        else:
            sends = [pick_half(h, axis_at, 1 - mine) for h in held]
            stacked = jax.tree.map(lambda *xs: jnp.stack(xs), *sends)
            stacked = swap_relabelled(stacked, axis, bit)
            got = [jax.tree.map(lambda x: x[r], stacked) for r in range(len(roots))]
        new_held = []
        for r, root in enumerate(roots):
            holder = ((me ^ root) & (full & ~done_mask)) == 0
            keep = pick_half(held[r], axis_at, mine)
            new_held.append(
                jax.tree.map(lambda k, g: jnp.where(holder, k, g), keep, got[r])
            )
        held = new_held
        shared = False
        done_mask |= 1 << bit
    return held


def gather_all(pieces, axis, order, lead=0, relabelled=False):
    nbits = len(order)
    count = lax.axis_size(axis)
    me = lax.axis_index(axis)
    if relabelled:
        me = relabel(me, count)
    held = pieces
    for bit in order:
        axis_at = lead + nbits - 1 - bit
        mine = (me >> bit) & 1
        if relabelled:
            got = swap_relabelled(held, axis, bit)
        else:
            got = swap(held, axis, 1 << bit)

        def join(h, g):
            both = jnp.concatenate([h, h], axis=axis_at)
            return lax.dynamic_update_slice_in_dim(both, g, (1 - mine) * h.shape[axis_at], axis_at)

        held = jax.tree.map(join, held, got)
    return held


def sum_all(value, axis):
    count = lax.axis_size(axis)
    me = lax.axis_index(axis)
    total = lax.dynamic_index_in_dim(value, me, 0, keepdims=False)
    for mask in range(1, count):
        sent = lax.dynamic_index_in_dim(value, me ^ mask, 0, keepdims=False)
        total = total + swap(sent, axis, mask)
    result = jnp.zeros_like(value)
    result = lax.dynamic_update_index_in_dim(result, total, me, 0)
    for mask in range(1, count):
        got = swap(total, axis, mask)
        result = lax.dynamic_update_index_in_dim(result, got, me ^ mask, 0)
    return result


def contract_kernel(block, group, q_ref, perm_ref, mov_ref, out_ref):
    slots, local, waves = perm_ref.shape[1:]

    def some_slots(g, acc):
        first = g * group
        rows = perm_ref[0, pl.ds(first, group)].reshape(group * local, waves)
        product = jnp.dot(rows, mov_ref[0], preferred_element_type=jnp.float32)
        for j in range(group):
            part = product[j * local:(j + 1) * local]
            acc = acc + pltpu.roll(part, q_ref[first + j] * block, 1)
        return acc

    acc = lax.fori_loop(0, slots // group, some_slots, jnp.zeros(out_ref.shape[1:], jnp.float32))
    out_ref[0] = acc.astype(out_ref.dtype)


def contract(q_slots, permuted, moving, block):
    steps, slots, local, waves = permuted.shape
    cols = moving.shape[2]
    return pl.pallas_call(
        functools.partial(contract_kernel, block, 8 if slots % 8 == 0 else 1),
        out_shape=jax.ShapeDtypeStruct((steps, local, cols), jnp.bfloat16),
        grid_spec=pltpu.PrefetchScalarGridSpec(
            num_scalar_prefetch=1,
            grid=(steps,),
            in_specs=[
                pl.BlockSpec((1, slots, local, waves), lambda i, q: (i, 0, 0, 0)),
                pl.BlockSpec((1, waves, cols), lambda i, q: (i, 0, 0)),
            ],
            out_specs=pl.BlockSpec((1, local, cols), lambda i, q: (i, 0, 0)),
        ),
        cost_estimate=pl.CostEstimate(
            flops=2 * steps * slots * cols * local * waves,
            bytes_accessed=2 * steps * (slots * local * waves + cols * waves + cols * local),
            transcendentals=0,
        ),
    )(q_slots, permuted, moving)


def body(offsets, q_slots, forms, vectors, energies, screened, umklapp):
    kpoint_count = vectors.shape[0]
    vector_count = vectors.shape[1]
    pair_count = vectors.shape[2]
    local_waves = forms.shape[2]
    slot_count = screened.shape[2]
    plane_waves = screened.shape[3]
    step_count = offsets.shape[0]
    ka_size = lax.axis_size("ka")
    ga_size = lax.axis_size("ga")
    ka_bits = ka_size.bit_length() - 1
    ga_bits = ga_size.bit_length() - 1
    me_ka = lax.axis_index("ka")

    projected = lax.dot_general(
        vectors, forms, (((2,), (1,)), ((0,), (0,))), preferred_element_type=jnp.float32
    ).astype(jnp.bfloat16)

    per_piece = slot_count // ka_size
    slab = jnp.transpose(screened[0], (1, 0, 2))
    slab = slab.reshape((2,) * ka_bits + (per_piece, local_waves, plane_waves))
    table = umklapp[0].reshape((2,) * ka_bits + (per_piece, plane_waves))
    roots = [offsets[i] for i in range(step_count)]
    pieces = scatter_from_roots((slab, table), roots, "ka", list(range(ka_bits)))
    waves = jnp.arange(plane_waves, dtype=jnp.int32)
    permuted_pieces = []
    for piece, rows in pieces:
        piece = piece.reshape(per_piece, local_waves, plane_waves)
        rows = rows.reshape(per_piece, plane_waves)
        onehot = (rows[:, :, None] == waves[None, None, :]).astype(jnp.bfloat16)
        moved_cols = lax.dot_general(
            piece, onehot, (((2,), (1,)), ((0,), (0,))), preferred_element_type=jnp.float32
        ).astype(jnp.bfloat16)
        permuted_pieces.append(
            moved_cols.reshape((1,) * ka_bits + (per_piece, local_waves, plane_waves))
        )
    gathered = gather_all(
        jnp.stack(permuted_pieces), "ka", list(range(ka_bits))[::-1], lead=1, relabelled=True
    )

    odd = [roots[i] & 1 for i in range(step_count)]
    hopped = from_behind(projected, "ka", 1)
    moving = [jnp.where(odd[i] == 1, hopped, projected) for i in range(step_count)]
    even_part = [roots[i] - odd[i] for i in range(step_count)]
    amounts = [
        jnp.where(me_ka & 1 == 0, even_part[i], (ka_size - even_part[i]) % ka_size)
        for i in range(step_count)
    ]
    for level in range(1, ka_bits):
        by = 1 << level
        pairs = [
            (j, (j + by) % ka_size if j % 2 == 0 else (j - by) % ka_size) for j in range(ka_size)
        ]
        hopped = lax.ppermute(jnp.stack(moving), "ka", pairs)
        moving = [
            jnp.where(amounts[i] >> level & 1 == 1, hopped[i], moving[i])
            for i in range(step_count)
        ]
    moving = jnp.stack(moving).reshape(step_count, kpoint_count * vector_count, local_waves)
    moving = jnp.transpose(moving, (0, 2, 1)).reshape(
        (step_count,) + (1,) * ga_bits + (local_waves, kpoint_count * vector_count)
    )
    ga_order = [0, 2, 1] if ga_bits == 3 else list(range(ga_bits))
    moving_all = gather_all(moving, "ga", ga_order, lead=1).reshape(
        step_count, plane_waves, kpoint_count * vector_count
    )

    permuted_all = gathered.reshape(step_count, slot_count, local_waves, plane_waves)
    kernel_part = contract(q_slots, permuted_all, moving_all, vector_count)
    kernel_part = kernel_part.reshape(step_count, local_waves, kpoint_count, vector_count)
    kernel_cat = jnp.concatenate([kernel_part[i] for i in range(step_count)], axis=2)
    action = lax.dot_general(
        kernel_cat, forms, (((0,), (2,)), ((1,), (0,))), preferred_element_type=jnp.float32
    )
    action = action.reshape(kpoint_count, step_count, vector_count, pair_count).sum(axis=1)
    action = action.reshape(ga_size, kpoint_count // ga_size, vector_count, pair_count)
    action = sum_all(action, "ga").reshape(kpoint_count, vector_count, pair_count)
    return energies[:, None, :] * vectors.astype(jnp.float32) - action


def solution(mesh):
    return jax.shard_map(
        body,
        mesh=mesh,
        in_specs=(
            P(),
            P(),
            P("ka", None, "ga"),
            P("ka", None, None),
            P("ka", None),
            P("ka", "ga", None, None),
            P("ka", None, None),
        ),
        out_specs=P("ka", None, None),
        check_vma=False,
    )
```

```python
import functools

import jax
import jax.numpy as jnp
from jax import lax
from jax.experimental import pallas as pl
from jax.experimental.pallas import tpu as pltpu
from jax.sharding import PartitionSpec as P


def from_behind(value, axis, by):
    count = lax.axis_size(axis)
    return lax.ppermute(value, axis, [(i, (i + by) % count) for i in range(count)])


def swap(value, axis, bit):
    count = lax.axis_size(axis)
    return lax.ppermute(value, axis, [(i, i ^ bit) for i in range(count)])


def relabel(index, size):
    if size < 8:
        return index
    one = (index >> 1) & 1
    two = (index >> 2) & 1
    swapped = index + (two - one) * 2 + (one - two) * 4
    if isinstance(index, int):
        return swapped if index & 1 else index
    return jnp.where(index & 1 == 1, swapped, index)


def swap_relabelled(value, axis, bit):
    count = lax.axis_size(axis)
    pairs = []
    for i in range(count):
        v = relabel(i, count) ^ (1 << bit)
        pairs.append((i, [j for j in range(count) if relabel(j, count) == v][0]))
    return lax.ppermute(value, axis, pairs)


def pick_half(tree, axis_at, which):
    return jax.tree.map(lambda a: lax.dynamic_slice_in_dim(a, which, 1, axis=axis_at), tree)


def scatter_from_roots(own, roots, axis, order):
    nbits = len(order)
    count = lax.axis_size(axis)
    me = relabel(lax.axis_index(axis), count)
    roots = [relabel(root, count) for root in roots]
    full = (1 << nbits) - 1
    held = [own] * len(roots)
    shared = True
    done_mask = 0
    for bit in order:
        axis_at = nbits - 1 - bit
        mine = (me >> bit) & 1
        if shared:
            sends = pick_half(own, axis_at, 1 - mine)
            got = swap_relabelled(sends, axis, bit)
            got = [got] * len(roots)
        else:
            sends = [pick_half(h, axis_at, 1 - mine) for h in held]
            stacked = jax.tree.map(lambda *xs: jnp.stack(xs), *sends)
            stacked = swap_relabelled(stacked, axis, bit)
            got = [jax.tree.map(lambda x: x[r], stacked) for r in range(len(roots))]
        new_held = []
        for r, root in enumerate(roots):
            holder = ((me ^ root) & (full & ~done_mask)) == 0
            keep = pick_half(held[r], axis_at, mine)
            new_held.append(
                jax.tree.map(lambda k, g: jnp.where(holder, k, g), keep, got[r])
            )
        held = new_held
        shared = False
        done_mask |= 1 << bit
    return held


def gather_all(pieces, axis, order, lead=0, relabelled=False):
    nbits = len(order)
    count = lax.axis_size(axis)
    me = lax.axis_index(axis)
    if relabelled:
        me = relabel(me, count)
    held = pieces
    for bit in order:
        axis_at = lead + nbits - 1 - bit
        mine = (me >> bit) & 1
        if relabelled:
            got = swap_relabelled(held, axis, bit)
        else:
            got = swap(held, axis, 1 << bit)

        def join(h, g):
            low = jnp.where(mine == 0, h, g)
            high = jnp.where(mine == 0, g, h)
            return jnp.concatenate([low, high], axis=axis_at)

        held = jax.tree.map(join, held, got)
    return held


def sum_all(value, axis):
    count = lax.axis_size(axis)
    me = lax.axis_index(axis)
    total = lax.dynamic_index_in_dim(value, me, 0, keepdims=False)
    for mask in range(1, count):
        sent = lax.dynamic_index_in_dim(value, me ^ mask, 0, keepdims=False)
        total = total + swap(sent, axis, mask)
    result = jnp.zeros_like(value)
    result = lax.dynamic_update_index_in_dim(result, total, me, 0)
    for mask in range(1, count):
        got = swap(total, axis, mask)
        result = lax.dynamic_update_index_in_dim(result, got, me ^ mask, 0)
    return result


def contract_kernel(block, group, q_ref, perm_ref, mov_ref, out_ref):
    slots, local, waves = perm_ref.shape[1:]

    def some_slots(g, acc):
        first = g * group
        rows = perm_ref[0, pl.ds(first, group)].reshape(group * local, waves)
        product = jnp.dot(rows, mov_ref[0], preferred_element_type=jnp.float32)
        for j in range(group):
            part = product[j * local:(j + 1) * local]
            acc = acc + pltpu.roll(part, q_ref[first + j] * block, 1)
        return acc

    acc = lax.fori_loop(0, slots // group, some_slots, jnp.zeros(out_ref.shape[1:], jnp.float32))
    out_ref[0] = acc.astype(out_ref.dtype)


def contract(q_slots, permuted, moving, block):
    steps, slots, local, waves = permuted.shape
    cols = moving.shape[2]
    return pl.pallas_call(
        functools.partial(contract_kernel, block, 16 if slots % 16 == 0 else 1),
        out_shape=jax.ShapeDtypeStruct((steps, local, cols), jnp.bfloat16),
        grid_spec=pltpu.PrefetchScalarGridSpec(
            num_scalar_prefetch=1,
            grid=(steps,),
            in_specs=[
                pl.BlockSpec((1, slots, local, waves), lambda i, q: (i, 0, 0, 0)),
                pl.BlockSpec((1, waves, cols), lambda i, q: (i, 0, 0)),
            ],
            out_specs=pl.BlockSpec((1, local, cols), lambda i, q: (i, 0, 0)),
        ),
        cost_estimate=pl.CostEstimate(
            flops=2 * steps * slots * cols * local * waves,
            bytes_accessed=2 * steps * (slots * local * waves + cols * waves + cols * local),
            transcendentals=0,
        ),
    )(q_slots, permuted, moving)


def body(offsets, q_slots, forms, vectors, energies, screened, umklapp):
    kpoint_count = vectors.shape[0]
    vector_count = vectors.shape[1]
    pair_count = vectors.shape[2]
    local_waves = forms.shape[2]
    slot_count = screened.shape[2]
    plane_waves = screened.shape[3]
    step_count = offsets.shape[0]
    ka_size = lax.axis_size("ka")
    ga_size = lax.axis_size("ga")
    ka_bits = ka_size.bit_length() - 1
    ga_bits = ga_size.bit_length() - 1
    me_ka = lax.axis_index("ka")

    projected = lax.dot_general(
        vectors, forms, (((2,), (1,)), ((0,), (0,))), preferred_element_type=jnp.float32
    ).astype(jnp.bfloat16)

    per_piece = slot_count // ka_size
    slab = jnp.transpose(screened[0], (1, 0, 2))
    slab = slab.reshape((2,) * ka_bits + (per_piece, local_waves, plane_waves))
    table = umklapp[0].reshape((2,) * ka_bits + (per_piece, plane_waves))
    roots = [offsets[i] for i in range(step_count)]
    pieces = scatter_from_roots((slab, table), roots, "ka", list(range(ka_bits)))
    waves = jnp.arange(plane_waves, dtype=jnp.int32)
    permuted_pieces = []
    for piece, rows in pieces:
        piece = piece.reshape(per_piece, local_waves, plane_waves)
        rows = rows.reshape(per_piece, plane_waves)
        onehot = (rows[:, :, None] == waves[None, None, :]).astype(jnp.bfloat16)
        moved_cols = lax.dot_general(
            piece, onehot, (((2,), (1,)), ((0,), (0,))), preferred_element_type=jnp.float32
        ).astype(jnp.bfloat16)
        permuted_pieces.append(
            moved_cols.reshape((1,) * ka_bits + (per_piece, local_waves, plane_waves))
        )
    gathered = gather_all(
        jnp.stack(permuted_pieces), "ka", list(range(ka_bits))[::-1], lead=1, relabelled=True
    )

    odd = [roots[i] & 1 for i in range(step_count)]
    hopped = from_behind(projected, "ka", 1)
    moving = [jnp.where(odd[i] == 1, hopped, projected) for i in range(step_count)]
    even_part = [roots[i] - odd[i] for i in range(step_count)]
    amounts = [
        jnp.where(me_ka & 1 == 0, even_part[i], (ka_size - even_part[i]) % ka_size)
        for i in range(step_count)
    ]
    for level in range(1, ka_bits):
        by = 1 << level
        pairs = [
            (j, (j + by) % ka_size if j % 2 == 0 else (j - by) % ka_size) for j in range(ka_size)
        ]
        hopped = lax.ppermute(jnp.stack(moving), "ka", pairs)
        moving = [
            jnp.where(amounts[i] >> level & 1 == 1, hopped[i], moving[i])
            for i in range(step_count)
        ]
    moving = jnp.stack(moving).reshape(step_count, kpoint_count * vector_count, local_waves)
    moving = jnp.transpose(moving, (0, 2, 1)).reshape(
        (step_count,) + (1,) * ga_bits + (local_waves, kpoint_count * vector_count)
    )
    ga_order = [0, 2, 1] if ga_bits == 3 else list(range(ga_bits))
    moving_all = gather_all(moving, "ga", ga_order, lead=1).reshape(
        step_count, plane_waves, kpoint_count * vector_count
    )

    permuted_all = gathered.reshape(step_count, slot_count, local_waves, plane_waves)
    kernel_part = contract(q_slots, permuted_all, moving_all, vector_count)
    kernel_part = kernel_part.reshape(step_count, local_waves, kpoint_count, vector_count)
    kernel_cat = jnp.concatenate([kernel_part[i] for i in range(step_count)], axis=2)
    action = lax.dot_general(
        kernel_cat, forms, (((0,), (2,)), ((1,), (0,))), preferred_element_type=jnp.float32
    )
    action = action.reshape(kpoint_count, step_count, vector_count, pair_count).sum(axis=1)
    action = action.reshape(ga_size, kpoint_count // ga_size, vector_count, pair_count)
    action = sum_all(action, "ga").reshape(kpoint_count, vector_count, pair_count)
    return energies[:, None, :] * vectors.astype(jnp.float32) - action


def solution(mesh):
    return jax.shard_map(
        body,
        mesh=mesh,
        in_specs=(
            P(),
            P(),
            P("ka", None, "ga"),
            P("ka", None, None),
            P("ka", None),
            P("ka", "ga", None, None),
            P("ka", None, None),
        ),
        out_specs=P("ka", None, None),
        check_vma=False,
    )
```

```python
import functools

import jax
import jax.numpy as jnp
from jax import lax
from jax.experimental import pallas as pl
from jax.experimental.pallas import tpu as pltpu
from jax.sharding import PartitionSpec as P


def from_behind(value, axis, by):
    count = lax.axis_size(axis)
    return lax.ppermute(value, axis, [(i, (i + by) % count) for i in range(count)])


def swap(value, axis, bit):
    count = lax.axis_size(axis)
    return lax.ppermute(value, axis, [(i, i ^ bit) for i in range(count)])


def relabel(index, size):
    if size < 8:
        return index
    one = (index >> 1) & 1
    two = (index >> 2) & 1
    swapped = index + (two - one) * 2 + (one - two) * 4
    if isinstance(index, int):
        return swapped if index & 1 else index
    return jnp.where(index & 1 == 1, swapped, index)


def swap_relabelled(value, axis, bit):
    count = lax.axis_size(axis)
    pairs = []
    for i in range(count):
        v = relabel(i, count) ^ (1 << bit)
        pairs.append((i, [j for j in range(count) if relabel(j, count) == v][0]))
    return lax.ppermute(value, axis, pairs)


def pick_half(tree, axis_at, which):
    return jax.tree.map(lambda a: lax.dynamic_slice_in_dim(a, which, 1, axis=axis_at), tree)


def scatter_from_roots(own, roots, axis, order):
    nbits = len(order)
    count = lax.axis_size(axis)
    me = relabel(lax.axis_index(axis), count)
    roots = [relabel(root, count) for root in roots]
    full = (1 << nbits) - 1
    held = [own] * len(roots)
    shared = True
    done_mask = 0
    for bit in order:
        axis_at = nbits - 1 - bit
        mine = (me >> bit) & 1
        if shared:
            sends = pick_half(own, axis_at, 1 - mine)
            got = swap_relabelled(sends, axis, bit)
            got = [got] * len(roots)
        else:
            sends = [pick_half(h, axis_at, 1 - mine) for h in held]
            stacked = jax.tree.map(lambda *xs: jnp.stack(xs), *sends)
            stacked = swap_relabelled(stacked, axis, bit)
            got = [jax.tree.map(lambda x: x[r], stacked) for r in range(len(roots))]
        new_held = []
        for r, root in enumerate(roots):
            holder = ((me ^ root) & (full & ~done_mask)) == 0
            keep = pick_half(held[r], axis_at, mine)
            new_held.append(
                jax.tree.map(lambda k, g: jnp.where(holder, k, g), keep, got[r])
            )
        held = new_held
        shared = False
        done_mask |= 1 << bit
    return held


def gather_all(pieces, axis, order, lead=0, relabelled=False):
    nbits = len(order)
    count = lax.axis_size(axis)
    me = lax.axis_index(axis)
    if relabelled:
        me = relabel(me, count)
    held = pieces
    for bit in order:
        axis_at = lead + nbits - 1 - bit
        mine = (me >> bit) & 1
        if relabelled:
            got = swap_relabelled(held, axis, bit)
        else:
            got = swap(held, axis, 1 << bit)

        def join(h, g):
            low = jnp.where(mine == 0, h, g)
            high = jnp.where(mine == 0, g, h)
            return jnp.concatenate([low, high], axis=axis_at)

        held = jax.tree.map(join, held, got)
    return held


def sum_all(value, axis):
    count = lax.axis_size(axis)
    me = lax.axis_index(axis)
    total = lax.dynamic_index_in_dim(value, me, 0, keepdims=False)
    for mask in range(1, count):
        sent = lax.dynamic_index_in_dim(value, me ^ mask, 0, keepdims=False)
        total = total + swap(sent, axis, mask)
    result = jnp.zeros_like(value)
    result = lax.dynamic_update_index_in_dim(result, total, me, 0)
    for mask in range(1, count):
        got = swap(total, axis, mask)
        result = lax.dynamic_update_index_in_dim(result, got, me ^ mask, 0)
    return result


def contract_kernel(block, group, q_ref, perm_ref, mov_ref, out_ref):
    slots, local, waves = perm_ref.shape[1:]

    def some_slots(g, acc):
        first = g * group
        rows = perm_ref[0, pl.ds(first, group)].reshape(group * local, waves)
        product = jnp.dot(rows, mov_ref[0], preferred_element_type=jnp.float32)
        for j in range(group):
            part = product[j * local:(j + 1) * local]
            acc = acc + pltpu.roll(part, q_ref[first + j] * block, 1)
        return acc

    acc = lax.fori_loop(0, slots // group, some_slots, jnp.zeros(out_ref.shape[1:], jnp.float32))
    out_ref[0] = acc.astype(out_ref.dtype)


def contract(q_slots, permuted, moving, block):
    steps, slots, local, waves = permuted.shape
    cols = moving.shape[2]
    return pl.pallas_call(
        functools.partial(contract_kernel, block, 32 if slots % 32 == 0 else 1),
        out_shape=jax.ShapeDtypeStruct((steps, local, cols), jnp.bfloat16),
        grid_spec=pltpu.PrefetchScalarGridSpec(
            num_scalar_prefetch=1,
            grid=(steps,),
            in_specs=[
                pl.BlockSpec((1, slots, local, waves), lambda i, q: (i, 0, 0, 0)),
                pl.BlockSpec((1, waves, cols), lambda i, q: (i, 0, 0)),
            ],
            out_specs=pl.BlockSpec((1, local, cols), lambda i, q: (i, 0, 0)),
        ),
        cost_estimate=pl.CostEstimate(
            flops=2 * steps * slots * cols * local * waves,
            bytes_accessed=2 * steps * (slots * local * waves + cols * waves + cols * local),
            transcendentals=0,
        ),
    )(q_slots, permuted, moving)


def body(offsets, q_slots, forms, vectors, energies, screened, umklapp):
    kpoint_count = vectors.shape[0]
    vector_count = vectors.shape[1]
    pair_count = vectors.shape[2]
    local_waves = forms.shape[2]
    slot_count = screened.shape[2]
    plane_waves = screened.shape[3]
    step_count = offsets.shape[0]
    ka_size = lax.axis_size("ka")
    ga_size = lax.axis_size("ga")
    ka_bits = ka_size.bit_length() - 1
    ga_bits = ga_size.bit_length() - 1
    me_ka = lax.axis_index("ka")

    projected = lax.dot_general(
        vectors, forms, (((2,), (1,)), ((0,), (0,))), preferred_element_type=jnp.float32
    ).astype(jnp.bfloat16)

    per_piece = slot_count // ka_size
    slab = jnp.transpose(screened[0], (1, 0, 2))
    slab = slab.reshape((2,) * ka_bits + (per_piece, local_waves, plane_waves))
    table = umklapp[0].reshape((2,) * ka_bits + (per_piece, plane_waves))
    roots = [offsets[i] for i in range(step_count)]
    pieces = scatter_from_roots((slab, table), roots, "ka", list(range(ka_bits)))
    waves = jnp.arange(plane_waves, dtype=jnp.int32)
    permuted_pieces = []
    for piece, rows in pieces:
        piece = piece.reshape(per_piece, local_waves, plane_waves)
        rows = rows.reshape(per_piece, plane_waves)
        onehot = (rows[:, :, None] == waves[None, None, :]).astype(jnp.bfloat16)
        moved_cols = lax.dot_general(
            piece, onehot, (((2,), (1,)), ((0,), (0,))), preferred_element_type=jnp.float32
        ).astype(jnp.bfloat16)
        permuted_pieces.append(
            moved_cols.reshape((1,) * ka_bits + (per_piece, local_waves, plane_waves))
        )
    gathered = gather_all(
        jnp.stack(permuted_pieces), "ka", list(range(ka_bits))[::-1], lead=1, relabelled=True
    )

    odd = [roots[i] & 1 for i in range(step_count)]
    hopped = from_behind(projected, "ka", 1)
    moving = [jnp.where(odd[i] == 1, hopped, projected) for i in range(step_count)]
    even_part = [roots[i] - odd[i] for i in range(step_count)]
    amounts = [
        jnp.where(me_ka & 1 == 0, even_part[i], (ka_size - even_part[i]) % ka_size)
        for i in range(step_count)
    ]
    for level in range(1, ka_bits):
        by = 1 << level
        pairs = [
            (j, (j + by) % ka_size if j % 2 == 0 else (j - by) % ka_size) for j in range(ka_size)
        ]
        hopped = lax.ppermute(jnp.stack(moving), "ka", pairs)
        moving = [
            jnp.where(amounts[i] >> level & 1 == 1, hopped[i], moving[i])
            for i in range(step_count)
        ]
    moving = jnp.stack(moving).reshape(step_count, kpoint_count * vector_count, local_waves)
    moving = jnp.transpose(moving, (0, 2, 1)).reshape(
        (step_count,) + (1,) * ga_bits + (local_waves, kpoint_count * vector_count)
    )
    ga_order = [0, 2, 1] if ga_bits == 3 else list(range(ga_bits))
    moving_all = gather_all(moving, "ga", ga_order, lead=1).reshape(
        step_count, plane_waves, kpoint_count * vector_count
    )

    permuted_all = gathered.reshape(step_count, slot_count, local_waves, plane_waves)
    kernel_part = contract(q_slots, permuted_all, moving_all, vector_count)
    kernel_part = kernel_part.reshape(step_count, local_waves, kpoint_count, vector_count)
    kernel_cat = jnp.concatenate([kernel_part[i] for i in range(step_count)], axis=2)
    action = lax.dot_general(
        kernel_cat, forms, (((0,), (2,)), ((1,), (0,))), preferred_element_type=jnp.float32
    )
    action = action.reshape(kpoint_count, step_count, vector_count, pair_count).sum(axis=1)
    action = action.reshape(ga_size, kpoint_count // ga_size, vector_count, pair_count)
    action = sum_all(action, "ga").reshape(kpoint_count, vector_count, pair_count)
    return energies[:, None, :] * vectors.astype(jnp.float32) - action


def solution(mesh):
    return jax.shard_map(
        body,
        mesh=mesh,
        in_specs=(
            P(),
            P(),
            P("ka", None, "ga"),
            P("ka", None, None),
            P("ka", None),
            P("ka", "ga", None, None),
            P("ka", None, None),
        ),
        out_specs=P("ka", None, None),
        check_vma=False,
    )
```
